256 devices in a mesh: slab: 32 (over z_lo, y, core), grp: 8 (over z_hi, x).
Axes of the slice: x: 4, y: 4, z: 8 (z_hi: 2, z_lo: 4; z = z_hi * 4 + z_lo), core: 2. Of those that a mesh axis runs over, the one named last changes fastest.
Arguments:
- volume: float32 [64, 128, 32, 128], P(None, 'slab', 'grp'), may hold values from -6 to 6
- conv_fine: float32 [3, 3, 3, 64, 64], replicated, may hold values from -0.15625 to 0.15625
- down_first: float32 [2, 2, 2, 64, 128], replicated, may hold values from -0.25 to 0.25
- conv_middle: float32 [3, 3, 3, 128, 128], replicated, may hold values from -0.109375 to 0.109375
- down_second: float32 [2, 2, 2, 128, 256], P(None, None, None, None, 'grp'), may hold values from -0.1875 to 0.1875
- conv_coarse: float32 [3, 3, 3, 256, 512], P(None, None, None, None, 'grp'), may hold values from -0.078125 to 0.078125
Outputs:
- features: float32 [512, 32, 256], P('grp', 'slab')
The draws below stay inside these ranges and needn't reach their ends.
All inputs are finite; a program needn't handle non-finite values.
Results may differ from the reference program's by a relative error of at most 0.000082.
Values sent between devices are 32-bit elements; how exact they have to be, the bound alone decides.
No kernel may reach another device: no remote copies, remote signals or barrier semaphores. Data moves between devices by JAX's collectives and lax.ppermute only.
A program may use at most 64 MiB of HBM per device.

```python
import jax
import jax.numpy as jnp
from jax import lax

C1 = 64
C2 = 128
C3 = 256
C4 = 512
WIDTH = 128
DEPTH = 128
HEIGHT = 32


def shard_levels(key, dims, pieces, low, largest):
    factor_of = 1.0
    for dim, parts in pieces:
        steps = jax.random.uniform(jax.random.fold_in(jax.random.fold_in(key, 6), dim), (parts,), jnp.float32, low / len(pieces), largest / len(pieces))
        factor_of = factor_of * jnp.repeat(jnp.exp(steps), dims[dim] // parts).reshape((-1,) + (1,) * (len(dims) - 1 - dim))
    return factor_of


def scatter_about(own_key, extent, deviation, reach, pieces=(), dtype=jnp.bfloat16):
    values = deviation * jax.random.normal(own_key, extent, jnp.float32)
    if pieces:
        values = values * shard_levels(own_key, extent, pieces, -0.22, 0.18)
    return jnp.clip(values, -reach, reach).astype(dtype)


def setup_inputs(seed: int = 0) -> dict:
    keys = jax.random.split(jax.random.key(seed), 7)
    volume = scatter_about(keys[0], (C1, DEPTH, HEIGHT, WIDTH), 1.0, 6.0, ((1, 32), (2, 8)), jnp.float32)
    conv_fine = scatter_about(keys[1], (3, 3, 3, C1, C1), (27 * C1) ** -0.5, 0.15625, (), jnp.float32)
    down_first = scatter_about(keys[2], (2, 2, 2, C1, C2), (8 * C1) ** -0.5, 0.25, (), jnp.float32)
    conv_middle = scatter_about(keys[3], (3, 3, 3, C2, C2), (27 * C2) ** -0.5, 0.109375, (), jnp.float32)
    down_second = scatter_about(keys[4], (2, 2, 2, C2, C3), (8 * C2) ** -0.5, 0.1875, ((4, 8),), jnp.float32)
    conv_coarse = scatter_about(keys[5], (3, 3, 3, C3, C4), (27 * C3) ** -0.5, 0.078125, ((4, 8),), jnp.float32)
    return {"volume": volume, "conv_fine": conv_fine, "down_first": down_first, "conv_middle": conv_middle, "down_second": down_second, "conv_coarse": conv_coarse}


def convolve(field, kernel, stride, padding):
    return lax.conv_general_dilated(field[None], kernel, (stride, stride, stride), padding, dimension_numbers=("NCDHW", "DHWIO", "NCDHW"), precision=lax.Precision.HIGHEST)[0]


def reference(volume, conv_fine, down_first, conv_middle, down_second, conv_coarse):
    same = ((1, 1), (1, 1), (1, 1))
    valid = ((0, 0), (0, 0), (0, 0))
    level_one = jax.nn.gelu(convolve(volume, conv_fine, 1, same), approximate=False)
    level_two = convolve(level_one, down_first, 2, valid)
    level_two = jax.nn.gelu(convolve(level_two, conv_middle, 1, same), approximate=False)
    coarse = convolve(level_two, down_second, 2, valid)
    result = jax.nn.gelu(convolve(coarse, conv_coarse, 1, same), approximate=False)
    return result.reshape(C4, DEPTH // 4, (HEIGHT // 4) * (WIDTH // 4))
```

```python
import functools

import jax
import jax.numpy as jnp
from jax import lax
from jax.experimental import pallas as pl
from jax.experimental.pallas import tpu as pltpu
from jax.sharding import PartitionSpec as P

F32 = jnp.float32
BF16 = jnp.bfloat16
XORS = (0, 4, 1, 5, 2, 6, 3, 7)


def split(x):
    hi = x.astype(BF16)
    return hi, (x - hi.astype(F32)).astype(BF16)


def mm(a, b):
    return lax.dot_general(a, b, (((1,), (0,)), ((), ())), preferred_element_type=F32)


def mm_t(a, b):
    return lax.dot_general(a, b, (((1,), (1,)), ((), ())), preferred_element_type=F32)


def gelu(v):
    return v * (1.0 + lax.erf(v * 0.7071067811865476)) * 0.5


def call(kernel, outs, args, scratch=(), flops=0):
    vmem = pl.BlockSpec(memory_space=pltpu.VMEM)
    size = sum(a.size * a.dtype.itemsize for a in args)
    return pl.pallas_call(
        kernel,
        out_shape=[jax.ShapeDtypeStruct(s, t) for s, t in outs],
        in_specs=[vmem] * len(args),
        out_specs=[vmem] * len(outs),
        scratch_shapes=list(scratch),
        compiler_params=pltpu.CompilerParams(vmem_limit_bytes=16 * 2**20),
        cost_estimate=pl.CostEstimate(flops=flops, bytes_accessed=size, transcendentals=0),
        name=kernel.__name__,
    )(*args)


def edges(vol, w2, low, high, half):
    for d in range(4):
        low[d * 64 : d * 64 + 64, :] = vol[pl.ds(d * 4, 64, stride=16), :]
        high[d * 64 : d * 64 + 64, :] = vol[pl.ds(d * 4 + 3, 64, stride=16), :]
    part = lax.rem(lax.axis_index("slab"), 2)
    half[...] = w2[pl.ds(pl.multiple_of(part * 128, 128), 128), :]


def put_shifted(x, high, low, lead, row, lane):
    column = lax.broadcasted_iota(jnp.int32, x.shape, 1)
    for k in range(3):
        if k == 0:
            y = jnp.where(column == 0, 0.0, pltpu.roll(x, 1, 1))
        elif k == 1:
            y = x
        else:
            y = jnp.where(column == 127, 0.0, pltpu.roll(x, 127, 1))
        hi, lo = split(y)
        high[lead, row + 64 * k : row + 64 * k + 64, lane : lane + 128] = hi
        low[lead, row + 64 * k : row + 64 * k + 64, lane : lane + 128] = lo


def taps(weights, high, low):
    both = mm(weights, high)
    return both[:192] + both[192:] + mm(weights[:192], low)


def planes(first, second):
    by_depth = [first[:, :128], first[:, 128:], second[:, :128], second[:, 128:]]
    sums = []
    for out in range(-1, 5):
        terms = [by_depth[out + a - 1][a * 64 : a * 64 + 64] for a in range(3) if 0 <= out + a - 1 < 4]
        sums.append(functools.reduce(jnp.add, terms))
    return sums


def fine_own(vol, w1, acc, wt, high, low):
    zeros = jnp.zeros((64, 256), BF16)
    for lead in range(2):
        for h in range(4):
            high[lead, h * 256 + 192 : h * 256 + 256, :] = zeros
            low[lead, h * 256 + 192 : h * 256 + 256, :] = zeros
    for b in range(3):
        wt[:, b * 256 + 192 : b * 256 + 256] = jnp.zeros((384, 64), BF16)
    for a in range(3):
        for b in range(3):
            x = w1[a * 576 + b * 192 : a * 576 + b * 192 + 192, :]
            x = jnp.concatenate([x, jnp.zeros((64, 64), F32)], axis=0)
            hi, lo = split(x.T)
            wt[a * 64 : a * 64 + 64, b * 256 : b * 256 + 256] = hi
            wt[192 + a * 64 : 192 + a * 64 + 64, b * 256 : b * 256 + 256] = lo
    for d in range(4):
        for h in range(4):
            put_shifted(vol[pl.ds(d * 4 + h, 64, stride=16), :], high, low, d // 2, h * 256, d % 2 * 128)
    for h in range(4):
        first, last = max(h - 1, 0), min(h + 1, 3)
        rows = slice(first * 256, last * 256 + 256)
        lanes = slice((first - h + 1) * 256, (last - h + 2) * 256)
        weights = wt[:, lanes]
        parts = [taps(weights, high[lead, rows, :], low[lead, rows, :]) for lead in range(2)]
        for i, value in enumerate(planes(*parts)):
            acc[i * 256 + h * 64 : i * 256 + h * 64 + 64, :] = value


def fine_rim(acc, wt, below, above, inner, down, up, high, low):
    grp = lax.axis_index("grp")
    zeros = jnp.zeros((64, 256), BF16)
    for side in range(2):
        ref = (below, above)[side]
        h = (0, 3)[side]
        inside = (grp > 0, grp < lax.axis_size("grp") - 1)[side]
        for lead in range(2):
            high[lead, 192:256, :] = zeros
            low[lead, 192:256, :] = zeros
        for d in range(4):
            x = jnp.where(inside, ref[d * 64 : d * 64 + 64, :], 0.0)
            put_shifted(x, high, low, d // 2, 0, d % 2 * 128)
        weights = wt[:, side * 512 : side * 512 + 256]
        parts = [taps(weights, high[lead], low[lead]) for lead in range(2)]
        for i, value in enumerate(planes(*parts)):
            total = value + acc[i * 256 + h * 64 : i * 256 + h * 64 + 64, :]
            if i == 0:
                down[h * 64 : h * 64 + 64, :] = total
            elif i == 5:
                up[h * 64 : h * 64 + 64, :] = total
            else:
                at = (i - 1) * 128 + side * 64
                inner[at : at + 64, :] = total
    for h in (1, 2):
        down[h * 64 : h * 64 + 64, :] = acc[h * 64 : h * 64 + 64, :]
        up[h * 64 : h * 64 + 64, :] = acc[5 * 256 + h * 64 : 5 * 256 + h * 64 + 64, :]


def first_down(acc, inner, before, after, w, out_low, out_high, cells, whi, wlo):
    slab = lax.axis_index("slab")
    for a in range(2):
        for bk in range(4):
            hi, lo = split(w[(a * 4 + bk) * 64 : (a * 4 + bk) * 64 + 64, :])
            whi[(bk * 2 + a) * 64 : (bk * 2 + a) * 64 + 64, :] = hi
            wlo[(bk * 2 + a) * 64 : (bk * 2 + a) * 64 + 64, :] = lo
    for h in range(4):
        level = []
        for d in range(4):
            if h in (0, 3):
                at = d * 128 + (h == 3) * 64
                v = inner[at : at + 64, :]
            else:
                at = (d + 1) * 256 + h * 64
                v = acc[at : at + 64, :]
            if d == 0:
                v = v + jnp.where(slab > 0, before[h * 64 : h * 64 + 64, :], 0.0)
            if d == 3:
                v = v + jnp.where(slab < lax.axis_size("slab") - 1, after[h * 64 : h * 64 + 64, :], 0.0)
            level.append(gelu(v))
        for d2 in range(2):
            cells[h * 2 + d2] = jnp.concatenate(level[2 * d2 : 2 * d2 + 2], axis=0).T
    for h2 in range(2):
        rows = []
        for d2 in range(2):
            rows.append(jnp.concatenate(
                [cells[(2 * h2 + b) * 2 + d2, pl.ds(k, 64, stride=2), :] for b in range(2) for k in range(2)], axis=1))
        hi, lo = split(jnp.concatenate(rows, axis=0))
        both = mm(jnp.concatenate([hi, lo], axis=0), whi[...])
        (out_low, out_high)[h2][...] = both[:128] + both[128:] + mm(hi, wlo[...])


def filters(wm, wc, mid, coarse):
    for a in range(3):
        for i in range(9):
            x = wm[(a * 9 + i) * 128 : (a * 9 + i) * 128 + 128, :]
            hi, lo = split(x)
            mid[i * 128 : i * 128 + 128, a * 128 : a * 128 + 128] = hi
            mid[1152 + i * 128 : 1152 + i * 128 + 128, a * 128 : a * 128 + 128] = lo
            hi, lo = split(wc[(a * 9 + i) * 64 : (a * 9 + i) * 64 + 64, :])
            coarse[a * 64 : a * 64 + 64, i * 256 : i * 256 + 256] = hi
            coarse[192 + a * 64 : 192 + a * 64 + 64, i * 256 : i * 256 + 256] = lo


def gathered_filters(mine, other, whi, wlo):
    grp = lax.axis_index("grp")
    part = lax.rem(lax.axis_index("slab"), 2)
    for ref, half in ((mine, part), (other, 1 - part)):
        for j, mask in enumerate(XORS):
            at = pl.multiple_of((grp ^ mask) * 32, 32)
            for i in range(4):
                hi, lo = split(ref[j * 128 + i * 32 : j * 128 + i * 32 + 32, :])
                whi[half, pl.ds(at, 32), i * 128 : i * 128 + 128] = hi
                wlo[half, pl.ds(at, 32), i * 128 : i * 128 + 128] = lo


def shifted_rows(x, k, width):
    row = lax.rem(lax.broadcasted_iota(jnp.int32, x.shape, 0), width)
    if k == 0:
        return jnp.where(row == 0, 0.0, pltpu.roll(x, 1, 0))
    if k == 2:
        return jnp.where(row == width - 1, 0.0, pltpu.roll(x, x.shape[0] - 1, 0))
    return x


def middle(d_low, d_high, below, above, w, inner, down, up, high, low):
    grp = lax.axis_index("grp")
    for i, ref in enumerate((below, d_low, d_high, above)):
        for d in range(2):
            x = ref[d * 64 : d * 64 + 64, :]
            if i == 0:
                x = jnp.where(grp > 0, x, 0.0)
            if i == 3:
                x = jnp.where(grp < lax.axis_size("grp") - 1, x, 0.0)
            for k in range(3):
                hi, lo = split(shifted_rows(x, k, 64))
                high[d, i * 64 : i * 64 + 64, k * 128 : k * 128 + 128] = hi
                low[d, i * 64 : i * 64 + 64, k * 128 : k * 128 + 128] = lo
    total = jnp.zeros((256, 384), F32)
    for b in range(3):
        rows = slice(b * 64, b * 64 + 128)
        hi = [high[d, rows, :] for d in range(2)]
        lo = [low[d, rows, :] for d in range(2)]
        both = mm(jnp.concatenate(hi + lo, axis=0), w[b * 384 : b * 384 + 384, :])
        rest = mm(jnp.concatenate(hi, axis=0), w[1152 + b * 384 : 1152 + b * 384 + 384, :])
        total = total + (both[:256] + both[256:] + rest)
    inner[:128, :] = total[:128, 128:256] + total[128:, 256:]
    inner[128:, :] = total[:128, :128] + total[128:, 128:256]
    down[...] = total[:128, 256:]
    up[...] = total[128:, :128]


def second_down(inner, before, after, whi, wlo, out, cells):
    slab = lax.axis_index("slab")
    first = inner[:128, :] + jnp.where(slab > 0, before[...], 0.0)
    second = inner[128:, :] + jnp.where(slab < lax.axis_size("slab") - 1, after[...], 0.0)
    cells[:128, :] = gelu(first)
    cells[128:, :] = gelu(second)
    total = jnp.zeros((32, 256), F32)
    for a in range(2):
        x = jnp.concatenate(
            [cells[pl.ds(a * 128 + b * 64 + k, 32, stride=2), :] for b in range(2) for k in range(2)], axis=1)
        hi, lo = split(x)
        both = mm_t(jnp.concatenate([hi, lo], axis=0), whi[a])
        total = total + (both[:32] + both[32:] + mm_t(hi, wlo[a]))
    out[...] = total


def coarse_conv(own, one, two, three, w, down, mid, up, grid, high, low):
    grp = lax.axis_index("grp")
    base, x = grp & 4, grp & 3
    for r, ref in enumerate((own, one, two, three)):
        source = base + ((x - r) & 3)
        for j in range(2):
            at = pl.multiple_of((source ^ (4 * j)) * 32, 32)
            grid[pl.ds(at, 32), :] = ref[j * 32 : j * 32 + 32, :]
    zeros = jnp.zeros((32, 768), BF16)
    for ref in (high, low):
        ref[:32, :] = zeros
        ref[288:, :] = zeros
    for k in range(3):
        hi, lo = split(shifted_rows(grid[...], k, 32))
        high[32:288, k * 256 : k * 256 + 256] = hi
        low[32:288, k * 256 : k * 256 + 256] = lo
    total = jnp.zeros((192, 256), F32)
    for b in range(3):
        rows, lanes = slice(b * 32, b * 32 + 256), slice(b * 768, b * 768 + 768)
        both = mm_t(w[:, lanes], high[rows, :])
        total = total + (both[:192] + both[192:] + mm_t(w[:192, lanes], low[rows, :]))
    up[...] = total[:64]
    mid[...] = total[64:128]
    down[...] = total[128:]


def finish(mid, before, after, out):
    slab = lax.axis_index("slab")
    v = mid[...] + jnp.where(slab > 0, before[...], 0.0)
    v = v + jnp.where(slab < lax.axis_size("slab") - 1, after[...], 0.0)
    out[...] = gelu(v)


def per_device(volume, conv_fine, down_first, conv_middle, down_second, conv_coarse):
    slabs, grps = lax.axis_size("slab"), lax.axis_size("grp")

    def turn(x, axis, by):
        n = lax.axis_size(axis)
        return lax.ppermute(x, axis, [(i, (i + by) % n) for i in range(n)])

    def swap(x, axis, mask):
        n = lax.axis_size(axis)
        return lax.ppermute(x, axis, [(i, i ^ mask) for i in range(n)])

    def turn_x(x, by):
        return lax.ppermute(x, "grp", [(i, (i & 4) | ((i + by) & 3)) for i in range(grps)])

    vol = volume.reshape(1024, 128)
    w1 = conv_fine.reshape(1728, 64)
    wd1 = down_first.reshape(512, 128)
    wm = conv_middle.reshape(3456, 128)
    w2 = jnp.swapaxes(down_second, 3, 4).reshape(256, 128)
    wc = jnp.swapaxes(conv_coarse, 3, 4).reshape(1728, 256)

    low, high, half = call(edges, [((256, 128), F32), ((256, 128), F32), ((128, 128), F32)], (vol, w2))
    below, above = turn(high, "grp", 1), turn(low, "grp", -1)
    taken = [pltpu.VMEM((2, 1024, 256), BF16)] * 2
    acc, wt = call(fine_own, [((1536, 128), F32), ((384, 768), BF16)], (vol, w1), taken, flops=10**9)
    mid_w, coarse_w = call(filters, [((2304, 384), BF16), ((384, 2304), BF16)], (wm, wc), flops=10**8)

    two = jnp.concatenate([half, swap(half, "grp", 4)], axis=0)
    four = jnp.concatenate([two, swap(two, "grp", 1)], axis=0)
    mine = jnp.concatenate([four, swap(four, "grp", 2)], axis=0)
    other = swap(mine, "slab", 1)
    whi, wlo = call(gathered_filters, [((2, 256, 512), BF16)] * 2, (mine, other))

    inner, down, up = call(
        fine_rim, [((512, 128), F32), ((256, 128), F32), ((256, 128), F32)], (acc, wt, below, above),
        [pltpu.VMEM((2, 256, 256), BF16)] * 2, flops=10**8)
    before, after = turn(up, "slab", 1), turn(down, "slab", -1)
    d_low, d_high = call(
        first_down, [((128, 128), F32)] * 2, (acc, inner, before, after, wd1),
        [pltpu.VMEM((8, 128, 128), F32), pltpu.VMEM((512, 128), BF16), pltpu.VMEM((512, 128), BF16)], flops=10**8)
    below, above = turn(d_high, "grp", 1), turn(d_low, "grp", -1)
    inner, down, up = call(
        middle, [((256, 128), F32), ((128, 128), F32), ((128, 128), F32)], (d_low, d_high, below, above, mid_w),
        [pltpu.VMEM((2, 256, 384), BF16)] * 2, flops=10**8)
    before, after = turn(up, "slab", 1), turn(down, "slab", -1)
    (row,) = call(
        second_down, [((32, 256), F32)], (inner, before, after, whi, wlo), [pltpu.VMEM((256, 128), F32)], flops=10**8)
    pair = jnp.concatenate([row, swap(row, "grp", 4)], axis=0)
    others = [turn_x(pair, by) for by in (1, 2, 3)]
    down, mid, up = call(
        coarse_conv, [((64, 256), F32)] * 3, (pair, *others, coarse_w),
        [pltpu.VMEM((256, 256), F32), pltpu.VMEM((320, 768), BF16), pltpu.VMEM((320, 768), BF16)], flops=10**8)
    before, after = turn(up, "slab", 1), turn(down, "slab", -1)
    (out,) = call(finish, [((64, 256), F32)], (mid, before, after))
    return out.reshape(64, 1, 256)


def solution(mesh):
    placed = (
        P(None, "slab", "grp", None),
        P(),
        P(),
        P(),
        P(None, None, None, None, "grp"),
        P(None, None, None, None, "grp"),
    )
    return jax.shard_map(
        per_device, mesh=mesh, in_specs=placed, out_specs=P("grp", "slab", None), check_vma=False
    )
```

```python
import functools

import jax
import jax.numpy as jnp
from jax import lax
from jax.experimental import pallas as pl
from jax.experimental.pallas import tpu as pltpu
from jax.sharding import PartitionSpec as P

F32 = jnp.float32
BF16 = jnp.bfloat16
XORS = (0, 4, 1, 5, 3, 7, 2, 6)


def split(x):
    hi = x.astype(BF16)
    return hi, (x - hi.astype(F32)).astype(BF16)


def mm(a, b):
    return lax.dot_general(a, b, (((1,), (0,)), ((), ())), preferred_element_type=F32)


def mm_t(a, b):
    return lax.dot_general(a, b, (((1,), (1,)), ((), ())), preferred_element_type=F32)


def gelu(v):
    return v * (1.0 + lax.erf(v * 0.7071067811865476)) * 0.5


def call(kernel, outs, args, scratch=(), flops=0, after=()):
    vmem = pl.BlockSpec(memory_space=pltpu.VMEM)
    size = sum(a.size * a.dtype.itemsize for a in args)
    return pl.pallas_call(
        kernel,
        out_shape=[jax.ShapeDtypeStruct(s, t) for s, t in outs],
        in_specs=[vmem] * len(args) + [pl.BlockSpec(memory_space=pl.ANY)] * len(after),
        out_specs=[vmem] * len(outs),
        scratch_shapes=list(scratch),
        compiler_params=pltpu.CompilerParams(vmem_limit_bytes=16 * 2**20),
        cost_estimate=pl.CostEstimate(flops=flops, bytes_accessed=size, transcendentals=0),
        name=kernel.__name__,
    )(*args, *after)


def parity(axis):
    return lax.rem(lax.axis_index(axis), 2)


def send(near, far, index, up, down, axis):
    even = parity(axis) == 0
    near[index] = jnp.where(even, up, down)
    far[index] = jnp.where(even, down, up)


def received(near, far, index, axis):
    place = lax.axis_index(axis)
    even = parity(axis) == 0
    one, two = near[index], far[index]
    before = jnp.where(place > 0, jnp.where(even, two, one), 0.0)
    after = jnp.where(place < lax.axis_size(axis) - 1, jnp.where(even, one, two), 0.0)
    return before, after


def edges(vol, near, far):
    for d in range(4):
        first = vol[pl.ds(d * 4, 64, stride=16), :]
        last = vol[pl.ds(d * 4 + 3, 64, stride=16), :]
        send(near, far, pl.ds(d * 64, 64), last, first, "grp")


def own_half(w2, after, half):
    half[...] = w2[pl.ds(pl.multiple_of(parity("slab") * 128, 128), 128), :]


def joined(first, second, after, out):
    n = first.shape[0]
    out[:n, :] = first[...]
    out[n:, :] = second[...]


def put_shifted(x, high, low, lead, row, lane):
    column = lax.broadcasted_iota(jnp.int32, x.shape, 1)
    for k in range(3):
        if k == 0:
            y = jnp.where(column == 0, 0.0, pltpu.roll(x, 1, 1))
        elif k == 1:
            y = x
        else:
            y = jnp.where(column == 127, 0.0, pltpu.roll(x, 127, 1))
        hi, lo = split(y)
        high[lead, row + 64 * k : row + 64 * k + 64, lane : lane + 128] = hi
        low[lead, row + 64 * k : row + 64 * k + 64, lane : lane + 128] = lo


def taps(weights, high, low):
    both = mm(weights, high)
    return both[:192] + both[192:] + mm(weights[:192], low)


def planes(first, second):
    by_depth = [first[:, :128], first[:, 128:], second[:, :128], second[:, 128:]]
    sums = []
    for out in range(-1, 5):
        terms = [by_depth[out + a - 1][a * 64 : a * 64 + 64] for a in range(3) if 0 <= out + a - 1 < 4]
        sums.append(functools.reduce(jnp.add, terms))
    return sums


def fine_own(vol, w1, acc, wt, high, low):
    zeros = jnp.zeros((64, 256), BF16)
    for lead in range(2):
        for h in range(4):
            high[lead, h * 256 + 192 : h * 256 + 256, :] = zeros
            low[lead, h * 256 + 192 : h * 256 + 256, :] = zeros
    for b in range(3):
        wt[:, b * 256 + 192 : b * 256 + 256] = jnp.zeros((384, 64), BF16)
    for a in range(3):
        for b in range(3):
            x = w1[a * 576 + b * 192 : a * 576 + b * 192 + 192, :]
            x = jnp.concatenate([x, jnp.zeros((64, 64), F32)], axis=0)
            hi, lo = split(x.T)
            wt[a * 64 : a * 64 + 64, b * 256 : b * 256 + 256] = hi
            wt[192 + a * 64 : 192 + a * 64 + 64, b * 256 : b * 256 + 256] = lo
    for d in range(4):
        for h in range(4):
            put_shifted(vol[pl.ds(d * 4 + h, 64, stride=16), :], high, low, d // 2, h * 256, d % 2 * 128)
    for h in range(4):
        first, last = max(h - 1, 0), min(h + 1, 3)
        rows = slice(first * 256, last * 256 + 256)
        lanes = slice((first - h + 1) * 256, (last - h + 2) * 256)
        weights = wt[:, lanes]
        parts = [taps(weights, high[lead, rows, :], low[lead, rows, :]) for lead in range(2)]
        for i, value in enumerate(planes(*parts)):
            acc[i * 256 + h * 64 : i * 256 + h * 64 + 64, :] = value


def fine_rim(acc, wt, near, far, inner, out_near, out_far, high, low):
    zeros = jnp.zeros((64, 256), BF16)
    for side in range(2):
        for lead in range(2):
            high[side * 2 + lead, 192:256, :] = zeros
            low[side * 2 + lead, 192:256, :] = zeros
    for d in range(4):
        below, above = received(near, far, pl.ds(d * 64, 64), "grp")
        put_shifted(below, high, low, d // 2, 0, d % 2 * 128)
        put_shifted(above, high, low, 2 + d // 2, 0, d % 2 * 128)
    for side in range(2):
        h = (0, 3)[side]
        weights = wt[:, side * 512 : side * 512 + 256]
        parts = [taps(weights, high[side * 2 + lead], low[side * 2 + lead]) for lead in range(2)]
        totals = planes(*parts)
        for i, value in enumerate(totals):
            totals[i] = value + acc[i * 256 + h * 64 : i * 256 + h * 64 + 64, :]
            if 0 < i < 5:
                inner[(i - 1) * 128 + side * 64 : (i - 1) * 128 + side * 64 + 64, :] = totals[i]
        send(out_near, out_far, pl.ds(h * 64, 64), totals[5], totals[0], "slab")
    for h in (1, 2):
        at = pl.ds(h * 64, 64)
        send(out_near, out_far, at, acc[5 * 256 + h * 64 : 5 * 256 + h * 64 + 64, :], acc[at, :], "slab")


def first_down(acc, inner, near, far, w, out_low, out_high, out_near, out_far, cells, whi, wlo):
    for a in range(2):
        for bk in range(4):
            hi, lo = split(w[(a * 4 + bk) * 64 : (a * 4 + bk) * 64 + 64, :])
            whi[(bk * 2 + a) * 64 : (bk * 2 + a) * 64 + 64, :] = hi
            wlo[(bk * 2 + a) * 64 : (bk * 2 + a) * 64 + 64, :] = lo
    for h in range(4):
        before, after = received(near, far, pl.ds(h * 64, 64), "slab")
        level = []
        for d in range(4):
            if h in (0, 3):
                at = d * 128 + (h == 3) * 64
                v = inner[at : at + 64, :]
            else:
                at = (d + 1) * 256 + h * 64
                v = acc[at : at + 64, :]
            if d == 0:
                v = v + before
            if d == 3:
                v = v + after
            level.append(gelu(v))
        for d2 in range(2):
            cells[h * 2 + d2] = jnp.concatenate(level[2 * d2 : 2 * d2 + 2], axis=0).T
    results = []
    for h2 in range(2):
        rows = []
        for d2 in range(2):
            rows.append(jnp.concatenate(
                [cells[(2 * h2 + b) * 2 + d2, pl.ds(k, 64, stride=2), :] for b in range(2) for k in range(2)], axis=1))
        hi, lo = split(jnp.concatenate(rows, axis=0))
        both = mm(jnp.concatenate([hi, lo], axis=0), whi[...])
        results.append(both[:128] + both[128:] + mm(hi, wlo[...]))
    out_low[...], out_high[...] = results
    send(out_near, out_far, slice(None), results[1], results[0], "grp")


def filters(wm, wc, mid, coarse):
    for a in range(3):
        for i in range(9):
            x = wm[(a * 9 + i) * 128 : (a * 9 + i) * 128 + 128, :]
            hi, lo = split(x)
            mid[i * 128 : i * 128 + 128, a * 128 : a * 128 + 128] = hi
            mid[1152 + i * 128 : 1152 + i * 128 + 128, a * 128 : a * 128 + 128] = lo
            hi, lo = split(wc[(a * 9 + i) * 64 : (a * 9 + i) * 64 + 64, :])
            coarse[a * 64 : a * 64 + 64, i * 256 : i * 256 + 256] = hi
            coarse[192 + a * 64 : 192 + a * 64 + 64, i * 256 : i * 256 + 256] = lo


def gathered_filters(mine, other, whi, wlo):
    grp = lax.axis_index("grp")
    part = lax.rem(lax.axis_index("slab"), 2)
    for ref, half in ((mine, part), (other, 1 - part)):
        for j, mask in enumerate(XORS):
            at = pl.multiple_of((grp ^ mask) * 32, 32)
            for i in range(4):
                hi, lo = split(ref[j * 128 + i * 32 : j * 128 + i * 32 + 32, :])
                whi[half, pl.ds(at, 32), i * 128 : i * 128 + 128] = hi
                wlo[half, pl.ds(at, 32), i * 128 : i * 128 + 128] = lo


def shifted_rows(x, k, width):
    row = lax.rem(lax.broadcasted_iota(jnp.int32, x.shape, 0), width)
    if k == 0:
        return jnp.where(row == 0, 0.0, pltpu.roll(x, 1, 0))
    if k == 2:
        return jnp.where(row == width - 1, 0.0, pltpu.roll(x, x.shape[0] - 1, 0))
    return x


def put_rows(x, high, low, lead, row):
    for k in range(3):
        hi, lo = split(shifted_rows(x, k, 64))
        high[lead, row : row + 64, k * 128 : k * 128 + 128] = hi
        low[lead, row : row + 64, k * 128 : k * 128 + 128] = lo


def middle_taps(high, low, leads, rows, w, b):
    hi = [high[lead, rows, :] for lead in leads]
    lo = [low[lead, rows, :] for lead in leads]
    n = sum(x.shape[0] for x in hi)
    both = mm(jnp.concatenate(hi + lo, axis=0), w[b * 384 : b * 384 + 384, :])
    return both[:n] + both[n:] + mm(jnp.concatenate(hi, axis=0), w[1152 + b * 384 : 1152 + b * 384 + 384, :])


def middle_own(d_low, d_high, w, total, high, low):
    for i, ref in enumerate((d_low, d_high)):
        for d in range(2):
            put_rows(ref[d * 64 : d * 64 + 64, :], high, low, i, d * 64)
    every = slice(0, 128)
    center = middle_taps(high, low, (0, 1), every, w, 1)
    total[:128, :] = center[:128] + middle_taps(high, low, (1,), every, w, 2)
    total[128:, :] = center[128:] + middle_taps(high, low, (0,), every, w, 0)


def middle_rim(own, near, far, w, inner, out_near, out_far, high, low):
    for d in range(2):
        below, above = received(near, far, pl.ds(d * 64, 64), "grp")
        put_rows(below, high, low, 0, d * 64)
        put_rows(above, high, low, 1, d * 64)
    every = slice(0, 128)
    for h in range(2):
        total = own[h * 128 : h * 128 + 128, :] + middle_taps(high, low, (h,), every, w, 2 * h)
        inner[h * 64 : h * 64 + 64, :] = total[:64, 128:256] + total[64:, 256:]
        inner[128 + h * 64 : 128 + h * 64 + 64, :] = total[:64, :128] + total[64:, 128:256]
        send(out_near, out_far, pl.ds(h * 64, 64), total[64:, :128], total[:64, 256:], "slab")


def second_down(inner, near, far, whi, wlo, out, cells):
    before, after = received(near, far, slice(None), "slab")
    cells[:128, :] = gelu(inner[:128, :] + before)
    cells[128:, :] = gelu(inner[128:, :] + after)
    total = jnp.zeros((32, 256), F32)
    for a in range(2):
        x = jnp.concatenate(
            [cells[pl.ds(a * 128 + b * 64 + k, 32, stride=2), :] for b in range(2) for k in range(2)], axis=1)
        hi, lo = split(x)
        both = mm_t(jnp.concatenate([hi, lo], axis=0), whi[a])
        total = total + (both[:32] + both[32:] + mm_t(hi, wlo[a]))
    out[...] = total


def coarse_conv(own, one, two, three, w, mid, out_near, out_far, grid, high, low):
    grp = lax.axis_index("grp")
    for mask, ref in enumerate((own, one, two, three)):
        for j in range(2):
            at = pl.multiple_of((grp ^ (mask + 4 * j)) * 32, 32)
            grid[pl.ds(at, 32), :] = ref[j * 32 : j * 32 + 32, :]
    zeros = jnp.zeros((32, 768), BF16)
    for ref in (high, low):
        ref[:32, :] = zeros
        ref[288:, :] = zeros
    for k in range(3):
        hi, lo = split(shifted_rows(grid[...], k, 32))
        high[32:288, k * 256 : k * 256 + 256] = hi
        low[32:288, k * 256 : k * 256 + 256] = lo
    total = jnp.zeros((192, 256), F32)
    for b in range(3):
        rows, lanes = slice(b * 32, b * 32 + 256), slice(b * 768, b * 768 + 768)
        both = mm_t(w[:, lanes], high[rows, :])
        total = total + (both[:192] + both[192:] + mm_t(w[:192, lanes], low[rows, :]))
    mid[...] = total[64:128]
    send(out_near, out_far, slice(None), total[:64], total[128:], "slab")


def finish(mid, near, far, out):
    before, after = received(near, far, slice(None), "slab")
    out[:, 0, :] = gelu(mid[...] + before + after)


def per_device(volume, conv_fine, down_first, conv_middle, down_second, conv_coarse):
    slabs, grps = lax.axis_size("slab"), lax.axis_size("grp")

    def permute(x, target):
        pairs = []
        for s in range(slabs):
            for g in range(grps):
                t, u = target(s, g)
                pairs.append((s * grps + g, t * grps + u))
        return lax.ppermute(x, ("slab", "grp"), pairs)

    def far_slab(s, g):
        if s in (0, slabs - 1):
            return slabs - 1 - s, g ^ 4
        return (s + 1 if s % 2 else s - 1), g

    def far_grp(s, g):
        if g in (0, grps - 1):
            z, rest = divmod(s, slabs // 4)
            return (3 - z) * (slabs // 4) + rest, grps - 1 - g
        return s, (g + 1 if g % 2 else g - 1)

    def over_grp(near, far):
        return swap(near, "grp", 1), permute(far, far_grp)

    def over_slab(near, far):
        return swap(near, "slab", 1), permute(far, far_slab)

    def swap(x, axis, mask):
        if axis == "slab":
            return permute(x, lambda s, g: (s ^ mask, g))
        return permute(x, lambda s, g: (s, g ^ mask))

    def join(first, second, after):
        rows, lanes = first.shape
        return call(joined, [((2 * rows, lanes), F32)], (first, second), after=(after,))[0]

    vol = volume.reshape(1024, 128)
    w1 = conv_fine.reshape(1728, 64)
    wd1 = down_first.reshape(512, 128)
    wm = conv_middle.reshape(3456, 128)
    w2 = jnp.swapaxes(down_second, 3, 4).reshape(256, 128)
    wc = jnp.swapaxes(conv_coarse, 3, 4).reshape(1728, 256)

    rim = over_grp(*call(edges, [((256, 128), F32)] * 2, (vol,)))
    taken = [pltpu.VMEM((2, 1024, 256), BF16)] * 2
    acc, wt = call(fine_own, [((1536, 128), F32), ((384, 768), BF16)], (vol, w1), taken, flops=10**9)
    (half,) = call(own_half, [((128, 128), F32)], (w2,), after=(acc,))
    second = swap(half, "grp", 4)

    taken = [pltpu.VMEM((4, 256, 256), BF16)] * 2
    inner, *out = call(fine_rim, [((512, 128), F32)] + [((256, 128), F32)] * 2, (acc, wt, *rim), taken, flops=10**8)
    rim = over_slab(*out)
    two = join(half, second, inner)
    second = swap(two, "grp", 1)
    mid_w, coarse_w = call(filters, [((2304, 384), BF16), ((384, 2304), BF16)], (wm, wc), flops=10**8)

    taken = [pltpu.VMEM((8, 128, 128), F32), pltpu.VMEM((512, 128), BF16), pltpu.VMEM((512, 128), BF16)]
    d_low, d_high, *out = call(first_down, [((128, 128), F32)] * 4, (acc, inner, *rim, wd1), taken, flops=10**8)
    rim = over_grp(*out)
    four = join(two, second, d_low)
    second = swap(four, "grp", 3)
    taken = [pltpu.VMEM((2, 128, 384), BF16)] * 2
    (own,) = call(middle_own, [((256, 384), F32)], (d_low, d_high, mid_w), taken, flops=10**8)
    inner, *out = call(
        middle_rim, [((256, 128), F32)] + [((128, 128), F32)] * 2, (own, *rim, mid_w), taken, flops=10**8)
    rim = over_slab(*out)
    mine = join(four, second, inner)
    other = swap(mine, "slab", 1)
    whi, wlo = call(gathered_filters, [((2, 256, 512), BF16)] * 2, (mine, other))
    (row,) = call(
        second_down, [((32, 256), F32)], (inner, *rim, whi, wlo), [pltpu.VMEM((256, 128), F32)], flops=10**8)

    pair = join(row, swap(row, "grp", 4), row)
    others = [swap(pair, "grp", mask) for mask in (1, 2, 3)]
    taken = [pltpu.VMEM((256, 256), F32), pltpu.VMEM((320, 768), BF16), pltpu.VMEM((320, 768), BF16)]
    mid, *out = call(coarse_conv, [((64, 256), F32)] * 3, (pair, *others, coarse_w), taken, flops=10**8)
    rim = over_slab(*out)
    return call(finish, [((64, 1, 256), F32)], (mid, *rim))[0]


def solution(mesh):
    placed = (
        P(None, "slab", "grp", None),
        P(),
        P(),
        P(),
        P(None, None, None, None, "grp"),
        P(None, None, None, None, "grp"),
    )
    return jax.shard_map(
        per_device, mesh=mesh, in_specs=placed, out_specs=P("grp", "slab", None), check_vma=False
    )
```

```python
import functools

import jax
import jax.numpy as jnp
from jax import lax
from jax.experimental import pallas as pl
from jax.experimental.pallas import tpu as pltpu
from jax.sharding import PartitionSpec as P

F32 = jnp.float32
BF16 = jnp.bfloat16
XORS = (0, 4, 1, 5, 3, 7, 2, 6)


def split(x):
    hi = x.astype(BF16)
    return hi, (x - hi.astype(F32)).astype(BF16)


def mm(a, b):
    return lax.dot_general(a, b, (((1,), (0,)), ((), ())), preferred_element_type=F32)


def mm_t(a, b):
    return lax.dot_general(a, b, (((1,), (1,)), ((), ())), preferred_element_type=F32)


def gelu(v):
    return v * (1.0 + lax.erf(v * 0.7071067811865476)) * 0.5


def call(kernel, outs, args, scratch=(), flops=0, after=()):
    vmem = pl.BlockSpec(memory_space=pltpu.VMEM)
    size = sum(a.size * a.dtype.itemsize for a in args)
    n = len(args)

    def body(*refs):
        kernel(*refs[:n], *refs[n + len(after) :])

    return pl.pallas_call(
        body,
        out_shape=[jax.ShapeDtypeStruct(s, t) for s, t in outs],
        in_specs=[vmem] * len(args) + [pl.BlockSpec(memory_space=pl.ANY)] * len(after),
        out_specs=[vmem] * len(outs),
        scratch_shapes=list(scratch),
        compiler_params=pltpu.CompilerParams(vmem_limit_bytes=16 * 2**20),
        cost_estimate=pl.CostEstimate(flops=flops, bytes_accessed=size, transcendentals=0),
        name=kernel.__name__,
    )(*args, *after)


def parity(axis):
    return lax.rem(lax.axis_index(axis), 2)


def send(near, far, index, up, down, axis):
    even = parity(axis) == 0
    near[index] = jnp.where(even, up, down)
    far[index] = jnp.where(even, down, up)


def received(near, far, index, axis):
    place = lax.axis_index(axis)
    even = parity(axis) == 0
    one, two = near[index], far[index]
    before = jnp.where(place > 0, jnp.where(even, two, one), 0.0)
    after = jnp.where(place < lax.axis_size(axis) - 1, jnp.where(even, one, two), 0.0)
    return before, after


def edges(vol, near, far):
    for i in range(3):
        for d in range(4):
            low = vol[pl.ds(d * 4 + i, 64, stride=16), :]
            high = vol[pl.ds(d * 4 + i + 1, 64, stride=16), :]
            send(near, far, pl.ds((i * 4 + d) * 64, 64), high, low, "grp")


def own_half(w2, half):
    half[...] = w2[pl.ds(pl.multiple_of(parity("slab") * 128, 128), 128), :]


def joined(first, second, out):
    n = first.shape[0]
    out[:n, :] = first[...]
    out[n:, :] = second[...]


def put_shifted(x, high, low, lead, row, lane):
    column = lax.broadcasted_iota(jnp.int32, x.shape, 1)
    for k in range(3):
        if k == 0:
            y = jnp.where(column == 0, 0.0, pltpu.roll(x, 1, 1))
        elif k == 1:
            y = x
        else:
            y = jnp.where(column == 127, 0.0, pltpu.roll(x, 127, 1))
        hi, lo = split(y)
        high[lead, row + 64 * k : row + 64 * k + 64, lane : lane + 128] = hi
        low[lead, row + 64 * k : row + 64 * k + 64, lane : lane + 128] = lo


def taps(weights, high, low):
    both = mm(weights, high)
    return both[:192] + both[192:] + mm(weights[:192], low)


def planes(first, second):
    by_depth = [first[:, :128], first[:, 128:], second[:, :128], second[:, 128:]]
    sums = []
    for out in range(-1, 5):
        terms = [by_depth[out + a - 1][a * 64 : a * 64 + 64] for a in range(3) if 0 <= out + a - 1 < 4]
        sums.append(functools.reduce(jnp.add, terms))
    return sums


def fine_own(vol, w1, acc, wt, high, low):
    zeros = jnp.zeros((64, 256), BF16)
    for lead in range(2):
        for h in range(4):
            high[lead, h * 256 + 192 : h * 256 + 256, :] = zeros
            low[lead, h * 256 + 192 : h * 256 + 256, :] = zeros
    for b in range(3):
        wt[:, b * 256 + 192 : b * 256 + 256] = jnp.zeros((384, 64), BF16)
    for a in range(3):
        for b in range(3):
            x = w1[a * 576 + b * 192 : a * 576 + b * 192 + 192, :]
            x = jnp.concatenate([x, jnp.zeros((64, 64), F32)], axis=0)
            hi, lo = split(x.T)
            wt[a * 64 : a * 64 + 64, b * 256 : b * 256 + 256] = hi
            wt[192 + a * 64 : 192 + a * 64 + 64, b * 256 : b * 256 + 256] = lo
    for d in range(4):
        for h in range(4):
            put_shifted(vol[pl.ds(d * 4 + h, 64, stride=16), :], high, low, d // 2, h * 256, d % 2 * 128)
    for h in range(-1, 5):
        first, last = max(h - 1, 0), min(h + 1, 3)
        rows = slice(first * 256, last * 256 + 256)
        lanes = slice((first - h + 1) * 256, (last - h + 2) * 256)
        weights = wt[:, lanes]
        parts = [taps(weights, high[lead, rows, :], low[lead, rows, :]) for lead in range(2)]
        for i, value in enumerate(planes(*parts)):
            acc[i * 384 + h * 64 + 64 : i * 384 + h * 64 + 128, :] = value


def rim_sums(side, acc, wt, ref, inside, high, low):
    for i in range(3):
        for lead in range(2):
            high[lead, i * 256 + 192 : i * 256 + 256, :] = jnp.zeros((64, 256), BF16)
            low[lead, i * 256 + 192 : i * 256 + 256, :] = jnp.zeros((64, 256), BF16)
        for d in range(4):
            x = jnp.where(inside, ref[(i * 4 + d) * 64 : (i * 4 + d) * 64 + 64, :], 0.0)
            put_shifted(x, high, low, d // 2, i * 256, d % 2 * 128)
    found = []
    for j in range(3):
        h = (j - 2, j + 3)[side]
        first, last = (j, 2) if side == 0 else (0, j)
        rows = slice(first * 256, last * 256 + 256)
        tap = first - j if side == 0 else 2 - j
        weights = wt[:, tap * 256 : tap * 256 + (last - first + 1) * 256]
        sums = planes(*[taps(weights, high[lead, rows, :], low[lead, rows, :]) for lead in range(2)])
        if -1 <= h <= 4:
            sums = [v + acc[i * 384 + h * 64 + 64 : i * 384 + h * 64 + 128, :] for i, v in enumerate(sums)]
        found.append(sums)
    return found


def in_grp(side):
    place = lax.axis_index("grp")
    return place > 0 if side == 0 else place < lax.axis_size("grp") - 1


def fine_near(acc, wt, ref, out, high, low):
    for side in range(2):
        @pl.when(parity("grp") == 1 - side)
        def _():
            for j, sums in enumerate(rim_sums(side, acc, wt, ref, in_grp(side), high, low)):
                for i, value in enumerate(sums):
                    out[(i * 3 + j) * 64 : (i * 3 + j) * 64 + 64, :] = value


def fine_far(acc, wt, ref, other, inner, out_near, out_far, high, low):
    def put(h, sums):
        at = (h + 2) * 64
        send(out_near, out_far, pl.ds(at, 64), sums[5], sums[0], "slab")
        for d in range(4):
            inner[d * 512 + at : d * 512 + at + 64, :] = sums[d + 1]

    for side in range(2):
        @pl.when(parity("grp") == side)
        def _():
            for j, sums in enumerate(rim_sums(side, acc, wt, ref, in_grp(side), high, low)):
                put((j - 2, j + 3)[side], sums)
                put((j + 3, j - 2)[side], [other[(i * 3 + j) * 64 : (i * 3 + j) * 64 + 64, :] for i in range(6)])
    for h in (1, 2):
        put(h, [acc[i * 384 + h * 64 + 64 : i * 384 + h * 64 + 128, :] for i in range(6)])


def first_down(inner, near, far, w, out, cells, whi, wlo):
    for a in range(2):
        for bk in range(4):
            hi, lo = split(w[(a * 4 + bk) * 64 : (a * 4 + bk) * 64 + 64, :])
            whi[(bk * 2 + a) * 64 : (bk * 2 + a) * 64 + 64, :] = hi
            wlo[(bk * 2 + a) * 64 : (bk * 2 + a) * 64 + 64, :] = lo
    for h in range(8):
        before, after = received(near, far, pl.ds(h * 64, 64), "slab")
        level = [inner[d * 512 + h * 64 : d * 512 + h * 64 + 64, :] for d in range(4)]
        level = [gelu(v) for v in (level[0] + before, level[1], level[2], level[3] + after)]
        for d2 in range(2):
            cells[h * 2 + d2] = jnp.concatenate(level[2 * d2 : 2 * d2 + 2], axis=0).T
    for h2 in range(4):
        rows = []
        for d2 in range(2):
            rows.append(jnp.concatenate(
                [cells[(2 * h2 + b) * 2 + d2, pl.ds(k, 64, stride=2), :] for b in range(2) for k in range(2)], axis=1))
        hi, lo = split(jnp.concatenate(rows, axis=0))
        both = mm(jnp.concatenate([hi, lo], axis=0), whi[...])
        value = both[:128] + both[128:] + mm(hi, wlo[...])
        if h2 in (0, 3):
            value = jnp.where(in_grp(h2 // 3), value, 0.0)
        out[h2 * 128 : h2 * 128 + 128, :] = value


def filters(wm, wc, mid, coarse):
    for a in range(3):
        for i in range(9):
            x = wm[(a * 9 + i) * 128 : (a * 9 + i) * 128 + 128, :]
            hi, lo = split(x)
            mid[i * 128 : i * 128 + 128, a * 128 : a * 128 + 128] = hi
            mid[1152 + i * 128 : 1152 + i * 128 + 128, a * 128 : a * 128 + 128] = lo
            hi, lo = split(wc[(a * 9 + i) * 64 : (a * 9 + i) * 64 + 64, :])
            coarse[a * 64 : a * 64 + 64, i * 256 : i * 256 + 256] = hi
            coarse[192 + a * 64 : 192 + a * 64 + 64, i * 256 : i * 256 + 256] = lo


def gathered_filters(mine, other, whi, wlo):
    grp = lax.axis_index("grp")
    part = lax.rem(lax.axis_index("slab"), 2)
    for ref, half in ((mine, part), (other, 1 - part)):
        for j, mask in enumerate(XORS):
            at = pl.multiple_of((grp ^ mask) * 32, 32)
            for i in range(4):
                hi, lo = split(ref[j * 128 + i * 32 : j * 128 + i * 32 + 32, :])
                whi[half, pl.ds(at, 32), i * 128 : i * 128 + 128] = hi
                wlo[half, pl.ds(at, 32), i * 128 : i * 128 + 128] = lo


def shifted_rows(x, k, width):
    row = lax.rem(lax.broadcasted_iota(jnp.int32, x.shape, 0), width)
    if k == 0:
        return jnp.where(row == 0, 0.0, pltpu.roll(x, 1, 0))
    if k == 2:
        return jnp.where(row == width - 1, 0.0, pltpu.roll(x, x.shape[0] - 1, 0))
    return x


def middle(cells, w, inner, out_near, out_far, high, low):
    for h in range(4):
        for d in range(2):
            x = cells[h * 128 + d * 64 : h * 128 + d * 64 + 64, :]
            for k in range(3):
                hi, lo = split(shifted_rows(x, k, 64))
                high[d, h * 64 : h * 64 + 64, k * 128 : k * 128 + 128] = hi
                low[d, h * 64 : h * 64 + 64, k * 128 : k * 128 + 128] = lo
    total = jnp.zeros((256, 384), F32)
    for b in range(3):
        rows = slice(b * 64, b * 64 + 128)
        hi = [high[d, rows, :] for d in range(2)]
        lo = [low[d, rows, :] for d in range(2)]
        both = mm(jnp.concatenate(hi + lo, axis=0), w[b * 384 : b * 384 + 384, :])
        rest = mm(jnp.concatenate(hi, axis=0), w[1152 + b * 384 : 1152 + b * 384 + 384, :])
        total = total + (both[:256] + both[256:] + rest)
    inner[:128, :] = total[:128, 128:256] + total[128:, 256:]
    inner[128:, :] = total[:128, :128] + total[128:, 128:256]
    send(out_near, out_far, slice(None), total[128:, :128], total[:128, 256:], "slab")


def second_down(inner, near, far, whi, wlo, out, cells):
    before, after = received(near, far, slice(None), "slab")
    cells[:128, :] = gelu(inner[:128, :] + before)
    cells[128:, :] = gelu(inner[128:, :] + after)
    total = jnp.zeros((32, 256), F32)
    for a in range(2):
        x = jnp.concatenate(
            [cells[pl.ds(a * 128 + b * 64 + k, 32, stride=2), :] for b in range(2) for k in range(2)], axis=1)
        hi, lo = split(x)
        both = mm_t(jnp.concatenate([hi, lo], axis=0), whi[a])
        total = total + (both[:32] + both[32:] + mm_t(hi, wlo[a]))
    out[...] = total


def coarse_conv(own, one, two, three, w, mid, out_near, out_far, grid, high, low):
    grp = lax.axis_index("grp")
    for mask, ref in enumerate((own, one, two, three)):
        for j in range(2):
            at = pl.multiple_of((grp ^ (mask + 4 * j)) * 32, 32)
            grid[pl.ds(at, 32), :] = ref[j * 32 : j * 32 + 32, :]
    zeros = jnp.zeros((32, 768), BF16)
    for ref in (high, low):
        ref[:32, :] = zeros
        ref[288:, :] = zeros
    for k in range(3):
        hi, lo = split(shifted_rows(grid[...], k, 32))
        high[32:288, k * 256 : k * 256 + 256] = hi
        low[32:288, k * 256 : k * 256 + 256] = lo
    total = jnp.zeros((192, 256), F32)
    for b in range(3):
        rows, lanes = slice(b * 32, b * 32 + 256), slice(b * 768, b * 768 + 768)
        both = mm_t(w[:, lanes], high[rows, :])
        total = total + (both[:192] + both[192:] + mm_t(w[:192, lanes], low[rows, :]))
    mid[...] = total[64:128]
    send(out_near, out_far, slice(None), total[:64], total[128:], "slab")


def finish(mid, near, far, out):
    before, after = received(near, far, slice(None), "slab")
    v = gelu(mid[...] + before + after)
    for j in range(2):
        out[pl.ds(j, 64, stride=2), :] = v[:, j * 128 : j * 128 + 128]


def per_device(volume, conv_fine, down_first, conv_middle, down_second, conv_coarse):
    slabs, grps = lax.axis_size("slab"), lax.axis_size("grp")

    def permute(x, target):
        pairs = []
        for s in range(slabs):
            for g in range(grps):
                t, u = target(s, g)
                pairs.append((s * grps + g, t * grps + u))
        return lax.ppermute(x, ("slab", "grp"), pairs)

    def far_slab(s, g):
        if s in (0, slabs - 1):
            return slabs - 1 - s, g ^ 4
        return (s + 1 if s % 2 else s - 1), g

    def far_grp(s, g):
        if g in (0, grps - 1):
            z, rest = divmod(s, slabs // 4)
            return (3 - z) * (slabs // 4) + rest, grps - 1 - g
        return s, (g + 1 if g % 2 else g - 1)

    def over_grp(near, far):
        return swap(near, "grp", 1), permute(far, far_grp)

    def over_slab(near, far):
        return swap(near, "slab", 1), permute(far, far_slab)

    def swap(x, axis, mask):
        if axis == "slab":
            return permute(x, lambda s, g: (s ^ mask, g))
        return permute(x, lambda s, g: (s, g ^ mask))

    def join(first, second, after):
        rows, lanes = first.shape
        return call(joined, [((2 * rows, lanes), F32)], (first, second), after=(after,))[0]

    vol = volume.reshape(1024, 128)
    w1 = conv_fine.reshape(1728, 64)
    wd1 = down_first.reshape(512, 128)
    wm = conv_middle.reshape(3456, 128)
    w2 = jnp.swapaxes(down_second, 3, 4).reshape(256, 128)
    wc = jnp.swapaxes(conv_coarse, 3, 4).reshape(1728, 256)

    near, far = call(edges, [((768, 128), F32)] * 2, (vol,))
    (half,) = call(own_half, [((128, 128), F32)], (w2,), after=(near,))
    near, far = over_grp(near, far)
    taken = [pltpu.VMEM((2, 1024, 256), BF16)] * 2
    acc, wt = call(
        fine_own, [((2304, 128), F32), ((384, 768), BF16)], (vol, w1), taken, flops=10**9, after=(half,))
    second = swap(half, "grp", 4)
    taken = [pltpu.VMEM((2, 768, 256), BF16)] * 2
    (near,) = call(fine_near, [((1152, 128), F32)], (acc, wt, near), taken, flops=10**8)
    two = join(half, second, near)
    second = swap(two, "grp", 1)
    mid_w, coarse_w = call(filters, [((2304, 384), BF16), ((384, 2304), BF16)], (wm, wc), flops=10**8, after=(near,))
    inner, *out = call(
        fine_far, [((2048, 128), F32)] + [((512, 128), F32)] * 2, (acc, wt, far, near), taken, flops=10**8,
        after=(two, mid_w))
    rim = over_slab(*out)
    four = join(two, second, inner)
    second = swap(four, "grp", 3)

    taken = [pltpu.VMEM((16, 128, 128), F32), pltpu.VMEM((512, 128), BF16), pltpu.VMEM((512, 128), BF16)]
    (cells,) = call(first_down, [((512, 128), F32)], (inner, *rim, wd1), taken, flops=10**8)
    mine = join(four, second, cells)
    other = swap(mine, "slab", 1)
    taken = [pltpu.VMEM((2, 256, 384), BF16)] * 2
    inner, *out = call(
        middle, [((256, 128), F32)] + [((128, 128), F32)] * 2, (cells, mid_w), taken, flops=10**8)
    rim = over_slab(*out)
    whi, wlo = call(gathered_filters, [((2, 256, 512), BF16)] * 2, (mine, other))
    (row,) = call(
        second_down, [((32, 256), F32)], (inner, *rim, whi, wlo), [pltpu.VMEM((256, 128), F32)], flops=10**8)

    pair = join(row, swap(row, "grp", 4), row)
    others = [swap(pair, "grp", mask) for mask in (1, 2, 3)]
    taken = [pltpu.VMEM((256, 256), F32), pltpu.VMEM((320, 768), BF16), pltpu.VMEM((320, 768), BF16)]
    mid, *out = call(coarse_conv, [((64, 256), F32)] * 3, (pair, *others, coarse_w), taken, flops=10**8)
    rim = over_slab(*out)
    return call(finish, [((128, 128), F32)], (mid, *rim))[0].reshape(64, 1, 256)


def solution(mesh):
    placed = (
        P(None, "slab", "grp", None),
        P(),
        P(),
        P(),
        P(None, None, None, None, "grp"),
        P(None, None, None, None, "grp"),
    )
    return jax.shard_map(
        per_device, mesh=mesh, in_specs=placed, out_specs=P("grp", "slab", None), check_vma=False
    )
```

```python
import functools

import jax
import jax.numpy as jnp
from jax import lax
from jax.experimental import pallas as pl
from jax.experimental.pallas import tpu as pltpu
from jax.sharding import PartitionSpec as P

F32 = jnp.float32
BF16 = jnp.bfloat16
XORS = (0, 4, 1, 5, 3, 7, 2, 6)


def split(x):
    hi = x.astype(BF16)
    return hi, (x - hi.astype(F32)).astype(BF16)


def mm(a, b):
    return lax.dot_general(a, b, (((1,), (0,)), ((), ())), preferred_element_type=F32)


def mm_t(a, b):
    return lax.dot_general(a, b, (((1,), (1,)), ((), ())), preferred_element_type=F32)


def gelu(v):
    return v * (1.0 + lax.erf(v * 0.7071067811865476)) * 0.5


def call(kernel, outs, args, scratch=(), flops=0, after=(), spaces=None):
    vmem = pl.BlockSpec(memory_space=pltpu.VMEM)
    size = sum(a.size * a.dtype.itemsize for a in args)
    n = len(args)

    def body(*refs):
        kernel(*refs[:n], *refs[n + len(after) :])

    return pl.pallas_call(
        body,
        out_shape=[jax.ShapeDtypeStruct(s, t) for s, t in outs],
        in_specs=[pl.BlockSpec(memory_space=space) for space in spaces or (pltpu.VMEM,) * n] + [pl.BlockSpec(memory_space=pl.ANY)] * len(after),
        out_specs=[vmem] * len(outs),
        scratch_shapes=list(scratch),
        compiler_params=pltpu.CompilerParams(vmem_limit_bytes=16 * 2**20),
        cost_estimate=pl.CostEstimate(flops=flops, bytes_accessed=size, transcendentals=0),
        name=kernel.__name__,
    )(*args, *after)


def parity(axis):
    return lax.rem(lax.axis_index(axis), 2)


def send(near, far, index, up, down, axis):
    even = parity(axis) == 0
    near[index] = jnp.where(even, up, down)
    far[index] = jnp.where(even, down, up)


def received(near, far, index, axis):
    place = lax.axis_index(axis)
    even = parity(axis) == 0
    one, two = near[index], far[index]
    before = jnp.where(place > 0, jnp.where(even, two, one), 0.0)
    after = jnp.where(place < lax.axis_size(axis) - 1, jnp.where(even, one, two), 0.0)
    return before, after


def edges(vol, near, far):
    for d in range(4):
        first = vol[pl.ds(d * 4, 64, stride=16), :]
        last = vol[pl.ds(d * 4 + 3, 64, stride=16), :]
        send(near, far, pl.ds(d * 64, 64), last, first, "grp")


def own_half(w2, half):
    pltpu.sync_copy(w2.at[pl.ds(pl.multiple_of(parity("slab") * 128, 128), 128), :], half)


def joined(first, second, out):
    n = first.shape[0]
    out[:n, :] = first[...]
    out[n:, :] = second[...]


def put_shifted(x, high, low, lead, row, lane):
    column = lax.broadcasted_iota(jnp.int32, x.shape, 1)
    for k in range(3):
        if k == 0:
            y = jnp.where(column == 0, 0.0, pltpu.roll(x, 1, 1))
        elif k == 1:
            y = x
        else:
            y = jnp.where(column == 127, 0.0, pltpu.roll(x, 127, 1))
        hi, lo = split(y)
        high[lead, row + 64 * k : row + 64 * k + 64, lane : lane + 128] = hi
        low[lead, row + 64 * k : row + 64 * k + 64, lane : lane + 128] = lo


def taps(weights, high, low):
    both = mm(weights, high)
    return both[:192] + both[192:] + mm(weights[:192], low)


def planes(first, second):
    by_depth = [first[:, :128], first[:, 128:], second[:, :128], second[:, 128:]]
    sums = []
    for out in range(-1, 5):
        terms = [by_depth[out + a - 1][a * 64 : a * 64 + 64] for a in range(3) if 0 <= out + a - 1 < 4]
        sums.append(functools.reduce(jnp.add, terms))
    return sums


def fine_own(vol, w1, acc, wt, high, low):
    zeros = jnp.zeros((64, 256), BF16)
    for lead in range(2):
        for h in range(4):
            high[lead, h * 256 + 192 : h * 256 + 256, :] = zeros
            low[lead, h * 256 + 192 : h * 256 + 256, :] = zeros
    for b in range(3):
        wt[:, b * 256 + 192 : b * 256 + 256] = jnp.zeros((384, 64), BF16)
    for a in range(3):
        for b in range(3):
            x = w1[a * 576 + b * 192 : a * 576 + b * 192 + 192, :]
            x = jnp.concatenate([x, jnp.zeros((64, 64), F32)], axis=0)
            hi, lo = split(x.T)
            wt[a * 64 : a * 64 + 64, b * 256 : b * 256 + 256] = hi
            wt[192 + a * 64 : 192 + a * 64 + 64, b * 256 : b * 256 + 256] = lo
    for d in range(4):
        for h in range(4):
            put_shifted(vol[pl.ds(d * 4 + h, 64, stride=16), :], high, low, d // 2, h * 256, d % 2 * 128)
    for h in range(4):
        first, last = max(h - 1, 0), min(h + 1, 3)
        rows = slice(first * 256, last * 256 + 256)
        lanes = slice((first - h + 1) * 256, (last - h + 2) * 256)
        weights = wt[:, lanes]
        parts = [taps(weights, high[lead, rows, :], low[lead, rows, :]) for lead in range(2)]
        for i, value in enumerate(planes(*parts)):
            acc[i * 256 + h * 64 : i * 256 + h * 64 + 64, :] = value


def fine_rim(acc, wt, near, far, inner, out_near, out_far, high, low):
    zeros = jnp.zeros((64, 256), BF16)
    for side in range(2):
        for lead in range(2):
            high[side * 2 + lead, 192:256, :] = zeros
            low[side * 2 + lead, 192:256, :] = zeros
    for d in range(4):
        below, above = received(near, far, pl.ds(d * 64, 64), "grp")
        put_shifted(below, high, low, d // 2, 0, d % 2 * 128)
        put_shifted(above, high, low, 2 + d // 2, 0, d % 2 * 128)
    for side in range(2):
        h = (0, 3)[side]
        weights = wt[:, side * 512 : side * 512 + 256]
        parts = [taps(weights, high[side * 2 + lead], low[side * 2 + lead]) for lead in range(2)]
        totals = planes(*parts)
        for i, value in enumerate(totals):
            totals[i] = value + acc[i * 256 + h * 64 : i * 256 + h * 64 + 64, :]
            if 0 < i < 5:
                inner[(i - 1) * 128 + side * 64 : (i - 1) * 128 + side * 64 + 64, :] = totals[i]
        send(out_near, out_far, pl.ds(h * 64, 64), totals[5], totals[0], "slab")
    for h in (1, 2):
        at = pl.ds(h * 64, 64)
        send(out_near, out_far, at, acc[5 * 256 + h * 64 : 5 * 256 + h * 64 + 64, :], acc[at, :], "slab")


def first_down(acc, inner, near, far, w, out_low, out_high, out_near, out_far, cells, whi, wlo):
    for a in range(2):
        for bk in range(4):
            hi, lo = split(w[(a * 4 + bk) * 64 : (a * 4 + bk) * 64 + 64, :])
            whi[(bk * 2 + a) * 64 : (bk * 2 + a) * 64 + 64, :] = hi
            wlo[(bk * 2 + a) * 64 : (bk * 2 + a) * 64 + 64, :] = lo
    for h in range(4):
        before, after = received(near, far, pl.ds(h * 64, 64), "slab")
        level = []
        for d in range(4):
            if h in (0, 3):
                at = d * 128 + (h == 3) * 64
                v = inner[at : at + 64, :]
            else:
                at = (d + 1) * 256 + h * 64
                v = acc[at : at + 64, :]
            if d == 0:
                v = v + before
            if d == 3:
                v = v + after
            level.append(gelu(v))
        for d2 in range(2):
            cells[h * 2 + d2] = jnp.concatenate(level[2 * d2 : 2 * d2 + 2], axis=0).T
    results = []
    for h2 in range(2):
        rows = []
        for d2 in range(2):
            rows.append(jnp.concatenate(
                [cells[(2 * h2 + b) * 2 + d2, pl.ds(k, 64, stride=2), :] for b in range(2) for k in range(2)], axis=1))
        hi, lo = split(jnp.concatenate(rows, axis=0))
        both = mm(jnp.concatenate([hi, lo], axis=0), whi[...])
        results.append(both[:128] + both[128:] + mm(hi, wlo[...]))
    out_low[...], out_high[...] = results
    send(out_near, out_far, slice(None), results[1], results[0], "grp")


def filters(wm, wc, mid, coarse):
    for a in range(3):
        for i in range(9):
            x = wm[(a * 9 + i) * 128 : (a * 9 + i) * 128 + 128, :]
            hi, lo = split(x)
            mid[i * 128 : i * 128 + 128, a * 128 : a * 128 + 128] = hi
            mid[1152 + i * 128 : 1152 + i * 128 + 128, a * 128 : a * 128 + 128] = lo
            hi, lo = split(wc[(a * 9 + i) * 64 : (a * 9 + i) * 64 + 64, :])
            coarse[a * 64 : a * 64 + 64, i * 256 : i * 256 + 256] = hi
            coarse[192 + a * 64 : 192 + a * 64 + 64, i * 256 : i * 256 + 256] = lo


def gathered_filters(mine, other, whi, wlo):
    grp = lax.axis_index("grp")
    part = lax.rem(lax.axis_index("slab"), 2)
    for ref, half in ((mine, part), (other, 1 - part)):
        for j, mask in enumerate(XORS):
            at = pl.multiple_of((grp ^ mask) * 32, 32)
            for i in range(4):
                hi, lo = split(ref[j * 128 + i * 32 : j * 128 + i * 32 + 32, :])
                whi[half, pl.ds(at, 32), i * 128 : i * 128 + 128] = hi
                wlo[half, pl.ds(at, 32), i * 128 : i * 128 + 128] = lo


def shifted_rows(x, k, width):
    row = lax.rem(lax.broadcasted_iota(jnp.int32, x.shape, 0), width)
    if k == 0:
        return jnp.where(row == 0, 0.0, pltpu.roll(x, 1, 0))
    if k == 2:
        return jnp.where(row == width - 1, 0.0, pltpu.roll(x, x.shape[0] - 1, 0))
    return x


def put_rows(x, high, low, lead, row):
    for k in range(3):
        hi, lo = split(shifted_rows(x, k, 64))
        high[lead, row : row + 64, k * 128 : k * 128 + 128] = hi
        low[lead, row : row + 64, k * 128 : k * 128 + 128] = lo


def middle_taps(high, low, leads, rows, w, b):
    hi = [high[lead, rows, :] for lead in leads]
    lo = [low[lead, rows, :] for lead in leads]
    n = sum(x.shape[0] for x in hi)
    both = mm(jnp.concatenate(hi + lo, axis=0), w[b * 384 : b * 384 + 384, :])
    return both[:n] + both[n:] + mm(jnp.concatenate(hi, axis=0), w[1152 + b * 384 : 1152 + b * 384 + 384, :])


def middle_own(d_low, d_high, w, total, high, low):
    for i, ref in enumerate((d_low, d_high)):
        for d in range(2):
            put_rows(ref[d * 64 : d * 64 + 64, :], high, low, i, d * 64)
    every = slice(0, 128)
    center = middle_taps(high, low, (0, 1), every, w, 1)
    total[:128, :] = center[:128] + middle_taps(high, low, (1,), every, w, 2)
    total[128:, :] = center[128:] + middle_taps(high, low, (0,), every, w, 0)


def middle_rim(own, near, far, w, inner, out_near, out_far, high, low):
    for d in range(2):
        below, above = received(near, far, pl.ds(d * 64, 64), "grp")
        put_rows(below, high, low, 0, d * 64)
        put_rows(above, high, low, 1, d * 64)
    every = slice(0, 128)
    for h in range(2):
        total = own[h * 128 : h * 128 + 128, :] + middle_taps(high, low, (h,), every, w, 2 * h)
        inner[h * 64 : h * 64 + 64, :] = total[:64, 128:256] + total[64:, 256:]
        inner[128 + h * 64 : 128 + h * 64 + 64, :] = total[:64, :128] + total[64:, 128:256]
        send(out_near, out_far, pl.ds(h * 64, 64), total[64:, :128], total[:64, 256:], "slab")


def second_down(inner, near, far, whi, wlo, out, cells):
    before, after = received(near, far, slice(None), "slab")
    cells[:128, :] = gelu(inner[:128, :] + before)
    cells[128:, :] = gelu(inner[128:, :] + after)
    total = jnp.zeros((32, 256), F32)
    for a in range(2):
        x = jnp.concatenate(
            [cells[pl.ds(a * 128 + b * 64 + k, 32, stride=2), :] for b in range(2) for k in range(2)], axis=1)
        hi, lo = split(x)
        both = mm_t(jnp.concatenate([hi, lo], axis=0), whi[a])
        total = total + (both[:32] + both[32:] + mm_t(hi, wlo[a]))
    out[...] = total


def coarse_conv(own, one, two, three, w, mid, out_near, out_far, grid, high, low):
    grp = lax.axis_index("grp")
    for mask, ref in enumerate((own, one, two, three)):
        for j in range(2):
            at = pl.multiple_of((grp ^ (mask + 4 * j)) * 32, 32)
            grid[pl.ds(at, 32), :] = ref[j * 32 : j * 32 + 32, :]
    zeros = jnp.zeros((32, 768), BF16)
    for ref in (high, low):
        ref[:32, :] = zeros
        ref[288:, :] = zeros
    for k in range(3):
        hi, lo = split(shifted_rows(grid[...], k, 32))
        high[32:288, k * 256 : k * 256 + 256] = hi
        low[32:288, k * 256 : k * 256 + 256] = lo
    total = jnp.zeros((192, 256), F32)
    for b in range(3):
        rows, lanes = slice(b * 32, b * 32 + 256), slice(b * 768, b * 768 + 768)
        both = mm_t(w[:, lanes], high[rows, :])
        total = total + (both[:192] + both[192:] + mm_t(w[:192, lanes], low[rows, :]))
    mid[...] = total[64:128]
    send(out_near, out_far, slice(None), total[:64], total[128:], "slab")


def finish(mid, near, far, out):
    before, after = received(near, far, slice(None), "slab")
    v = gelu(mid[...] + before + after)
    for j in range(2):
        out[pl.ds(j, 64, stride=2), :] = v[:, j * 128 : j * 128 + 128]


def per_device(volume, conv_fine, down_first, conv_middle, down_second, conv_coarse):
    slabs, grps = lax.axis_size("slab"), lax.axis_size("grp")

    def permute(x, target):
        pairs = []
        for s in range(slabs):
            for g in range(grps):
                t, u = target(s, g)
                pairs.append((s * grps + g, t * grps + u))
        return lax.ppermute(x, ("slab", "grp"), pairs)

    def far_slab(s, g):
        if s in (0, slabs - 1):
            return s, g ^ 1
        return (s + 1 if s % 2 else s - 1), g

    def far_grp(s, g):
        if g in (0, grps - 1):
            return s ^ 1, g
        return s, (g + 1 if g % 2 else g - 1)

    def over_grp(near, far):
        far = permute(far, far_grp)
        return swap(near, "grp", 1), far

    def over_slab(near, far):
        far = permute(far, far_slab)
        return swap(near, "slab", 1), far

    def swap(x, axis, mask):
        if axis == "slab":
            return permute(x, lambda s, g: (s ^ mask, g))
        return permute(x, lambda s, g: (s, g ^ mask))

    def join(first, second, *after):
        rows, lanes = first.shape
        return call(joined, [((2 * rows, lanes), F32)], (first, second), after=after)[0]

    vol = volume.reshape(1024, 128)
    w1 = conv_fine.reshape(1728, 64)
    wd1 = down_first.reshape(512, 128)
    wm = conv_middle.reshape(3456, 128)
    w2 = jnp.swapaxes(down_second, 3, 4).reshape(256, 128)
    wc = jnp.swapaxes(conv_coarse, 3, 4).reshape(1728, 256)

    (half,) = call(own_half, [((128, 128), F32)], (w2,), spaces=(pl.ANY,))
    second = swap(half, "grp", 4)
    rim = over_grp(*call(edges, [((256, 128), F32)] * 2, (vol,), after=(half,)))
    taken = [pltpu.VMEM((2, 1024, 256), BF16)] * 2
    acc, wt = call(fine_own, [((1536, 128), F32), ((384, 768), BF16)], (vol, w1), taken, flops=10**9)
    two = join(half, second, acc)
    second = swap(two, "grp", 1)
    taken = [pltpu.VMEM((4, 256, 256), BF16)] * 2
    inner, *out = call(
        fine_rim, [((512, 128), F32)] + [((256, 128), F32)] * 2, (acc, wt, *rim), taken, flops=10**8,
        after=(two,))
    rim = over_slab(*out)
    four = join(two, second, *rim)
    second = swap(four, "grp", 3)
    mid_w, coarse_w = call(filters, [((2304, 384), BF16), ((384, 2304), BF16)], (wm, wc), flops=10**8)

    taken = [pltpu.VMEM((8, 128, 128), F32), pltpu.VMEM((512, 128), BF16), pltpu.VMEM((512, 128), BF16)]
    d_low, d_high, *out = call(first_down, [((128, 128), F32)] * 4, (acc, inner, *rim, wd1), taken, flops=10**8)
    rim = over_grp(*out)
    taken = [pltpu.VMEM((2, 128, 384), BF16)] * 2
    (own,) = call(middle_own, [((256, 384), F32)], (d_low, d_high, mid_w), taken, flops=10**8)
    inner, *out = call(
        middle_rim, [((256, 128), F32)] + [((128, 128), F32)] * 2, (own, *rim, mid_w), taken, flops=10**8)
    rim = over_slab(*out)
    mine = join(four, second, inner)
    other = swap(mine, "slab", 1)
    whi, wlo = call(gathered_filters, [((2, 256, 512), BF16)] * 2, (mine, other))
    (row,) = call(
        second_down, [((32, 256), F32)], (inner, *rim, whi, wlo), [pltpu.VMEM((256, 128), F32)], flops=10**8)

    pair = join(row, swap(row, "grp", 4))
    others = [swap(pair, "grp", mask) for mask in (1, 2, 3)]
    taken = [pltpu.VMEM((256, 256), F32), pltpu.VMEM((320, 768), BF16), pltpu.VMEM((320, 768), BF16)]
    mid, *out = call(coarse_conv, [((64, 256), F32)] * 3, (pair, *others, coarse_w), taken, flops=10**8)
    rim = over_slab(*out)
    return call(finish, [((128, 128), F32)], (mid, *rim))[0].reshape(64, 1, 256)


def solution(mesh):
    placed = (
        P(None, "slab", "grp", None),
        P(),
        P(),
        P(),
        P(None, None, None, None, "grp"),
        P(None, None, None, None, "grp"),
    )
    return jax.shard_map(
        per_device, mesh=mesh, in_specs=placed, out_specs=P("grp", "slab", None), check_vma=False
    )
```

```python
import functools

import jax
import jax.numpy as jnp
from jax import lax
from jax.experimental import pallas as pl
from jax.experimental.pallas import tpu as pltpu
from jax.sharding import PartitionSpec as P

F32 = jnp.float32
BF16 = jnp.bfloat16
XORS = (0, 4, 1, 5, 3, 7, 2, 6)


def split(x):
    hi = x.astype(BF16)
    return hi, (x - hi.astype(F32)).astype(BF16)


def mm(a, b):
    return lax.dot_general(a, b, (((1,), (0,)), ((), ())), preferred_element_type=F32)


def mm_t(a, b):
    return lax.dot_general(a, b, (((1,), (1,)), ((), ())), preferred_element_type=F32)


def gelu(v):
    return v * (1.0 + lax.erf(v * 0.7071067811865476)) * 0.5


def call(kernel, outs, args, scratch=(), flops=0, after=(), spaces=None):
    vmem = pl.BlockSpec(memory_space=pltpu.VMEM)
    size = sum(a.size * a.dtype.itemsize for a in args)
    n = len(args)

    def body(*refs):
        kernel(*refs[:n], *refs[n + len(after) :])

    return pl.pallas_call(
        body,
        out_shape=[jax.ShapeDtypeStruct(s, t) for s, t in outs],
        in_specs=[pl.BlockSpec(memory_space=space) for space in spaces or (pltpu.VMEM,) * n] + [pl.BlockSpec(memory_space=pl.ANY)] * len(after),
        out_specs=[vmem] * len(outs),
        scratch_shapes=list(scratch),
        compiler_params=pltpu.CompilerParams(vmem_limit_bytes=16 * 2**20),
        cost_estimate=pl.CostEstimate(flops=flops, bytes_accessed=size, transcendentals=0),
        name=kernel.__name__,
    )(*args, *after)


def parity(axis):
    return lax.rem(lax.axis_index(axis), 2)


def send(near, far, index, up, down, axis):
    even = parity(axis) == 0
    near[index] = jnp.where(even, up, down)
    far[index] = jnp.where(even, down, up)


def received(near, far, index, axis):
    place = lax.axis_index(axis)
    even = parity(axis) == 0
    one, two = near[index], far[index]
    before = jnp.where(place > 0, jnp.where(even, two, one), 0.0)
    after = jnp.where(place < lax.axis_size(axis) - 1, jnp.where(even, one, two), 0.0)
    return before, after


def edges(vol, near, far):
    for d in range(4):
        first = vol[pl.ds(d * 4, 64, stride=16), :]
        last = vol[pl.ds(d * 4 + 3, 64, stride=16), :]
        send(near, far, pl.ds(d * 64, 64), last, first, "grp")


def own_half(w2, half):
    half[...] = w2[pl.ds(pl.multiple_of(parity("slab") * 128, 128), 128), :]


def joined(first, second, out):
    n = first.shape[0]
    out[:n, :] = first[...]
    out[n:, :] = second[...]


def put_shifted(x, high, low, lead, row, lane):
    column = lax.broadcasted_iota(jnp.int32, x.shape, 1)
    for k in range(3):
        if k == 0:
            y = jnp.where(column == 0, 0.0, pltpu.roll(x, 1, 1))
        elif k == 1:
            y = x
        else:
            y = jnp.where(column == 127, 0.0, pltpu.roll(x, 127, 1))
        hi, lo = split(y)
        high[lead, row + 64 * k : row + 64 * k + 64, lane : lane + 128] = hi
        low[lead, row + 64 * k : row + 64 * k + 64, lane : lane + 128] = lo


def taps(weights, high, low):
    both = mm(weights, high)
    return both[:192] + both[192:] + mm(weights[:192], low)


def planes(first, second):
    by_depth = [first[:, :128], first[:, 128:], second[:, :128], second[:, 128:]]
    sums = []
    for out in range(-1, 5):
        terms = [by_depth[out + a - 1][a * 64 : a * 64 + 64] for a in range(3) if 0 <= out + a - 1 < 4]
        sums.append(functools.reduce(jnp.add, terms))
    return sums


def fine_own(vol, w1, acc, wt, high, low):
    zeros = jnp.zeros((64, 256), BF16)
    for lead in range(2):
        for h in range(4):
            high[lead, h * 256 + 192 : h * 256 + 256, :] = zeros
            low[lead, h * 256 + 192 : h * 256 + 256, :] = zeros
    for b in range(3):
        wt[:, b * 256 + 192 : b * 256 + 256] = jnp.zeros((384, 64), BF16)
    for a in range(3):
        for b in range(3):
            x = w1[a * 576 + b * 192 : a * 576 + b * 192 + 192, :]
            x = jnp.concatenate([x, jnp.zeros((64, 64), F32)], axis=0)
            hi, lo = split(x.T)
            wt[a * 64 : a * 64 + 64, b * 256 : b * 256 + 256] = hi
            wt[192 + a * 64 : 192 + a * 64 + 64, b * 256 : b * 256 + 256] = lo
    for d in range(4):
        for h in range(4):
            put_shifted(vol[pl.ds(d * 4 + h, 64, stride=16), :], high, low, d // 2, h * 256, d % 2 * 128)
    for h in range(4):
        first, last = max(h - 1, 0), min(h + 1, 3)
        rows = slice(first * 256, last * 256 + 256)
        lanes = slice((first - h + 1) * 256, (last - h + 2) * 256)
        weights = wt[:, lanes]
        parts = [taps(weights, high[lead, rows, :], low[lead, rows, :]) for lead in range(2)]
        for i, value in enumerate(planes(*parts)):
            acc[i * 256 + h * 64 : i * 256 + h * 64 + 64, :] = value


def fine_rim(acc, wt, near, far, inner, out_near, out_far, high, low):
    zeros = jnp.zeros((64, 256), BF16)
    for side in range(2):
        for lead in range(2):
            high[side * 2 + lead, 192:256, :] = zeros
            low[side * 2 + lead, 192:256, :] = zeros
    for d in range(4):
        below, above = received(near, far, pl.ds(d * 64, 64), "grp")
        put_shifted(below, high, low, d // 2, 0, d % 2 * 128)
        put_shifted(above, high, low, 2 + d // 2, 0, d % 2 * 128)
    for side in range(2):
        h = (0, 3)[side]
        weights = wt[:, side * 512 : side * 512 + 256]
        parts = [taps(weights, high[side * 2 + lead], low[side * 2 + lead]) for lead in range(2)]
        totals = planes(*parts)
        for i, value in enumerate(totals):
            totals[i] = value + acc[i * 256 + h * 64 : i * 256 + h * 64 + 64, :]
            if 0 < i < 5:
                inner[(i - 1) * 128 + side * 64 : (i - 1) * 128 + side * 64 + 64, :] = totals[i]
        send(out_near, out_far, pl.ds(h * 64, 64), totals[5], totals[0], "slab")
    for h in (1, 2):
        at = pl.ds(h * 64, 64)
        send(out_near, out_far, at, acc[5 * 256 + h * 64 : 5 * 256 + h * 64 + 64, :], acc[at, :], "slab")


def first_down(acc, inner, near, far, w, out_low, out_high, out_near, out_far, cells, whi, wlo):
    for a in range(2):
        for bk in range(4):
            hi, lo = split(w[(a * 4 + bk) * 64 : (a * 4 + bk) * 64 + 64, :])
            whi[(bk * 2 + a) * 64 : (bk * 2 + a) * 64 + 64, :] = hi
            wlo[(bk * 2 + a) * 64 : (bk * 2 + a) * 64 + 64, :] = lo
    for h in range(4):
        before, after = received(near, far, pl.ds(h * 64, 64), "slab")
        level = []
        for d in range(4):
            if h in (0, 3):
                at = d * 128 + (h == 3) * 64
                v = inner[at : at + 64, :]
            else:
                at = (d + 1) * 256 + h * 64
                v = acc[at : at + 64, :]
            if d == 0:
                v = v + before
            if d == 3:
                v = v + after
            level.append(gelu(v))
        for d2 in range(2):
            cells[h * 2 + d2] = jnp.concatenate(level[2 * d2 : 2 * d2 + 2], axis=0).T
    results = []
    for h2 in range(2):
        rows = []
        for d2 in range(2):
            rows.append(jnp.concatenate(
                [cells[(2 * h2 + b) * 2 + d2, pl.ds(k, 64, stride=2), :] for b in range(2) for k in range(2)], axis=1))
        hi, lo = split(jnp.concatenate(rows, axis=0))
        both = mm(jnp.concatenate([hi, lo], axis=0), whi[...])
        results.append(both[:128] + both[128:] + mm(hi, wlo[...]))
    out_low[...], out_high[...] = results
    send(out_near, out_far, slice(None), results[1], results[0], "grp")


def filters(wm, wc, mid, coarse):
    for a in range(3):
        for i in range(9):
            x = wm[(a * 9 + i) * 128 : (a * 9 + i) * 128 + 128, :]
            hi, lo = split(x)
            mid[i * 128 : i * 128 + 128, a * 128 : a * 128 + 128] = hi
            mid[1152 + i * 128 : 1152 + i * 128 + 128, a * 128 : a * 128 + 128] = lo
            hi, lo = split(wc[(a * 9 + i) * 64 : (a * 9 + i) * 64 + 64, :])
            coarse[a * 64 : a * 64 + 64, i * 256 : i * 256 + 256] = hi
            coarse[192 + a * 64 : 192 + a * 64 + 64, i * 256 : i * 256 + 256] = lo


def gathered_filters(mine, other, whi, wlo):
    grp = lax.axis_index("grp")
    part = lax.rem(lax.axis_index("slab"), 2)
    for ref, half in ((mine, part), (other, 1 - part)):
        for j, mask in enumerate(XORS):
            at = pl.multiple_of((grp ^ mask) * 32, 32)
            for i in range(4):
                hi, lo = split(ref[j * 128 + i * 32 : j * 128 + i * 32 + 32, :])
                whi[half, pl.ds(at, 32), i * 128 : i * 128 + 128] = hi
                wlo[half, pl.ds(at, 32), i * 128 : i * 128 + 128] = lo


def shifted_rows(x, k, width):
    row = lax.rem(lax.broadcasted_iota(jnp.int32, x.shape, 0), width)
    if k == 0:
        return jnp.where(row == 0, 0.0, pltpu.roll(x, 1, 0))
    if k == 2:
        return jnp.where(row == width - 1, 0.0, pltpu.roll(x, x.shape[0] - 1, 0))
    return x


def put_rows(x, high, low, lead, row):
    for k in range(3):
        hi, lo = split(shifted_rows(x, k, 64))
        high[lead, row : row + 64, k * 128 : k * 128 + 128] = hi
        low[lead, row : row + 64, k * 128 : k * 128 + 128] = lo


def middle_taps(high, low, leads, rows, w, b):
    hi = [high[lead, rows, :] for lead in leads]
    lo = [low[lead, rows, :] for lead in leads]
    n = sum(x.shape[0] for x in hi)
    both = mm(jnp.concatenate(hi + lo, axis=0), w[b * 384 : b * 384 + 384, :])
    return both[:n] + both[n:] + mm(jnp.concatenate(hi, axis=0), w[1152 + b * 384 : 1152 + b * 384 + 384, :])


def middle_own(d_low, d_high, w, total, high, low):
    for i, ref in enumerate((d_low, d_high)):
        for d in range(2):
            put_rows(ref[d * 64 : d * 64 + 64, :], high, low, i, d * 64)
    every = slice(0, 128)
    center = middle_taps(high, low, (0, 1), every, w, 1)
    total[:128, :] = center[:128] + middle_taps(high, low, (1,), every, w, 2)
    total[128:, :] = center[128:] + middle_taps(high, low, (0,), every, w, 0)


def middle_rim(own, near, far, w, inner, out_near, out_far, high, low):
    for d in range(2):
        below, above = received(near, far, pl.ds(d * 64, 64), "grp")
        put_rows(below, high, low, 0, d * 64)
        put_rows(above, high, low, 1, d * 64)
    every = slice(0, 128)
    for h in range(2):
        total = own[h * 128 : h * 128 + 128, :] + middle_taps(high, low, (h,), every, w, 2 * h)
        inner[h * 64 : h * 64 + 64, :] = total[:64, 128:256] + total[64:, 256:]
        inner[128 + h * 64 : 128 + h * 64 + 64, :] = total[:64, :128] + total[64:, 128:256]
        send(out_near, out_far, pl.ds(h * 64, 64), total[64:, :128], total[:64, 256:], "slab")


def second_down(inner, near, far, whi, wlo, out, cells):
    before, after = received(near, far, slice(None), "slab")
    cells[:128, :] = gelu(inner[:128, :] + before)
    cells[128:, :] = gelu(inner[128:, :] + after)
    total = jnp.zeros((32, 256), F32)
    for a in range(2):
        x = jnp.concatenate(
            [cells[pl.ds(a * 128 + b * 64 + k, 32, stride=2), :] for b in range(2) for k in range(2)], axis=1)
        hi, lo = split(x)
        both = mm_t(jnp.concatenate([hi, lo], axis=0), whi[a])
        total = total + (both[:32] + both[32:] + mm_t(hi, wlo[a]))
    out[...] = total


def coarse_conv(own, one, two, three, w, mid, out_near, out_far, grid, high, low):
    grp = lax.axis_index("grp")
    for mask, ref in enumerate((own, one, two, three)):
        for j in range(2):
            at = pl.multiple_of((grp ^ (mask + 4 * j)) * 32, 32)
            grid[pl.ds(at, 32), :] = ref[j * 32 : j * 32 + 32, :]
    zeros = jnp.zeros((32, 768), BF16)
    for ref in (high, low):
        ref[:32, :] = zeros
        ref[288:, :] = zeros
    for k in range(3):
        hi, lo = split(shifted_rows(grid[...], k, 32))
        high[32:288, k * 256 : k * 256 + 256] = hi
        low[32:288, k * 256 : k * 256 + 256] = lo
    total = jnp.zeros((192, 256), F32)
    for b in range(3):
        rows, lanes = slice(b * 32, b * 32 + 256), slice(b * 768, b * 768 + 768)
        both = mm_t(w[:, lanes], high[rows, :])
        total = total + (both[:192] + both[192:] + mm_t(w[:192, lanes], low[rows, :]))
    mid[...] = total[64:128]
    send(out_near, out_far, slice(None), total[:64], total[128:], "slab")


def finish(mid, near, far, out):
    before, after = received(near, far, slice(None), "slab")
    v = gelu(mid[...] + before + after)
    for j in range(2):
        out[pl.ds(j, 64, stride=2), :] = v[:, j * 128 : j * 128 + 128]


def per_device(volume, conv_fine, down_first, conv_middle, down_second, conv_coarse):
    slabs, grps = lax.axis_size("slab"), lax.axis_size("grp")

    def permute(x, target):
        pairs = []
        for s in range(slabs):
            for g in range(grps):
                t, u = target(s, g)
                pairs.append((s * grps + g, t * grps + u))
        return lax.ppermute(x, ("slab", "grp"), pairs)

    def far_slab(s, g):
        if s in (0, slabs - 1):
            return s, g ^ 1
        return (s + 1 if s % 2 else s - 1), g

    def far_grp(s, g):
        if g in (0, grps - 1):
            return s ^ 1, g
        return s, (g + 1 if g % 2 else g - 1)

    def over_grp(near, far):
        far = permute(far, far_grp)
        return swap(near, "grp", 1), far

    def over_slab(near, far):
        far = permute(far, far_slab)
        return swap(near, "slab", 1), far

    def swap(x, axis, mask):
        if axis == "slab":
            return permute(x, lambda s, g: (s ^ mask, g))
        return permute(x, lambda s, g: (s, g ^ mask))

    def join(first, second, *after):
        rows, lanes = first.shape
        return call(joined, [((2 * rows, lanes), F32)], (first, second), after=after)[0]

    vol = volume.reshape(1024, 128)
    w1 = conv_fine.reshape(1728, 64)
    wd1 = down_first.reshape(512, 128)
    wm = conv_middle.reshape(3456, 128)
    w2 = jnp.swapaxes(down_second, 3, 4).reshape(256, 128)
    wc = jnp.swapaxes(conv_coarse, 3, 4).reshape(1728, 256)

    out = call(edges, [((256, 128), F32)] * 2, (vol,))
    (half,) = call(own_half, [((128, 128), F32)], (w2,), after=(out[0],))
    rim = over_grp(*out)
    second = swap(half, "grp", 4)
    taken = [pltpu.VMEM((2, 1024, 256), BF16)] * 2
    acc, wt = call(
        fine_own, [((1536, 128), F32), ((384, 768), BF16)], (vol, w1), taken, flops=10**9, after=(half,))
    taken = [pltpu.VMEM((4, 256, 256), BF16)] * 2
    inner, *out = call(
        fine_rim, [((512, 128), F32)] + [((256, 128), F32)] * 2, (acc, wt, *rim), taken, flops=10**8)
    rim = over_slab(*out)
    two = join(half, second, inner)
    second = swap(two, "grp", 1)
    four = join(two, second, *rim)
    second = swap(four, "grp", 3)
    mid_w, coarse_w = call(filters, [((2304, 384), BF16), ((384, 2304), BF16)], (wm, wc), flops=10**8)

    taken = [pltpu.VMEM((8, 128, 128), F32), pltpu.VMEM((512, 128), BF16), pltpu.VMEM((512, 128), BF16)]
    d_low, d_high, *out = call(first_down, [((128, 128), F32)] * 4, (acc, inner, *rim, wd1), taken, flops=10**8)
    rim = over_grp(*out)
    taken = [pltpu.VMEM((2, 128, 384), BF16)] * 2
    (own,) = call(middle_own, [((256, 384), F32)], (d_low, d_high, mid_w), taken, flops=10**8)
    inner, *out = call(
        middle_rim, [((256, 128), F32)] + [((128, 128), F32)] * 2, (own, *rim, mid_w), taken, flops=10**8)
    rim = over_slab(*out)
    mine = join(four, second, inner)
    other = swap(mine, "slab", 1)
    whi, wlo = call(gathered_filters, [((2, 256, 512), BF16)] * 2, (mine, other))
    (row,) = call(
        second_down, [((32, 256), F32)], (inner, *rim, whi, wlo), [pltpu.VMEM((256, 128), F32)], flops=10**8)

    pair = join(row, swap(row, "grp", 4))
    others = [swap(pair, "grp", mask) for mask in (1, 2, 3)]
    taken = [pltpu.VMEM((256, 256), F32), pltpu.VMEM((320, 768), BF16), pltpu.VMEM((320, 768), BF16)]
    mid, *out = call(coarse_conv, [((64, 256), F32)] * 3, (pair, *others, coarse_w), taken, flops=10**8)
    rim = over_slab(*out)
    return call(finish, [((128, 128), F32)], (mid, *rim))[0].reshape(64, 1, 256)


def solution(mesh):
    placed = (
        P(None, "slab", "grp", None),
        P(),
        P(),
        P(),
        P(None, None, None, None, "grp"),
        P(None, None, None, None, "grp"),
    )
    return jax.shard_map(
        per_device, mesh=mesh, in_specs=placed, out_specs=P("grp", "slab", None), check_vma=False
    )
```

```python
import functools

import jax
import jax.numpy as jnp
from jax import lax
from jax.experimental import pallas as pl
from jax.experimental.pallas import tpu as pltpu
from jax.sharding import PartitionSpec as P

F32 = jnp.float32
BF16 = jnp.bfloat16
XORS = (0, 4, 1, 5, 3, 7, 2, 6)


def split(x):
    hi = x.astype(BF16)
    return hi, (x - hi.astype(F32)).astype(BF16)


def mm(a, b):
    return lax.dot_general(a, b, (((1,), (0,)), ((), ())), preferred_element_type=F32)


def mm_t(a, b):
    return lax.dot_general(a, b, (((1,), (1,)), ((), ())), preferred_element_type=F32)


def gelu(v):
    return v * (1.0 + lax.erf(v * 0.7071067811865476)) * 0.5


def call(kernel, outs, args, scratch=(), flops=0, after=(), spaces=None):
    vmem = pl.BlockSpec(memory_space=pltpu.VMEM)
    size = sum(a.size * a.dtype.itemsize for a in args)
    n = len(args)

    def body(*refs):
        kernel(*refs[:n], *refs[n + len(after) :])

    return pl.pallas_call(
        body,
        out_shape=[jax.ShapeDtypeStruct(s, t) for s, t in outs],
        in_specs=[pl.BlockSpec(memory_space=space) for space in spaces or (pltpu.VMEM,) * n] + [pl.BlockSpec(memory_space=pl.ANY)] * len(after),
        out_specs=[vmem] * len(outs),
        scratch_shapes=list(scratch),
        compiler_params=pltpu.CompilerParams(vmem_limit_bytes=16 * 2**20),
        cost_estimate=pl.CostEstimate(flops=flops, bytes_accessed=size, transcendentals=0),
        name=getattr(kernel, "__name__", "joined"),
    )(*args, *after)


def parity(axis):
    return lax.rem(lax.axis_index(axis), 2)


def send(near, far, index, up, down, axis):
    even = parity(axis) == 0
    near[index] = jnp.where(even, up, down)
    far[index] = jnp.where(even, down, up)


def received(near, far, index, axis):
    place = lax.axis_index(axis)
    even = parity(axis) == 0
    one, two = near[index], far[index]
    before = jnp.where(place > 0, jnp.where(even, two, one), 0.0)
    after = jnp.where(place < lax.axis_size(axis) - 1, jnp.where(even, one, two), 0.0)
    return before, after


def edges(vol, near, far):
    for d in range(4):
        first = vol[pl.ds(d * 4, 64, stride=16), :]
        last = vol[pl.ds(d * 4 + 3, 64, stride=16), :]
        send(near, far, pl.ds(d * 64, 64), last, first, "grp")
    far[256:, :] = jnp.zeros((8, 128), F32)


def own_half(w2, half):
    half[...] = w2[pl.ds(pl.multiple_of(parity("slab") * 128, 128), 128), :]


def joined(first, second, out, n):
    out[:n, :] = first[:n, :]
    out[n : 2 * n, :] = second[:n, :]
    if out.shape[0] > 2 * n:
        out[2 * n :, :] = jnp.zeros((out.shape[0] - 2 * n, out.shape[1]), F32)


def put_shifted(x, high, low, lead, row, lane):
    column = lax.broadcasted_iota(jnp.int32, x.shape, 1)
    for k in range(3):
        if k == 0:
            y = jnp.where(column == 0, 0.0, pltpu.roll(x, 1, 1))
        elif k == 1:
            y = x
        else:
            y = jnp.where(column == 127, 0.0, pltpu.roll(x, 127, 1))
        hi, lo = split(y)
        high[lead, row + 64 * k : row + 64 * k + 64, lane : lane + 128] = hi
        low[lead, row + 64 * k : row + 64 * k + 64, lane : lane + 128] = lo


def taps(weights, high, low):
    both = mm(weights, high)
    return both[:192] + both[192:] + mm(weights[:192], low)


def planes(first, second):
    by_depth = [first[:, :128], first[:, 128:], second[:, :128], second[:, 128:]]
    sums = []
    for out in range(-1, 5):
        terms = [by_depth[out + a - 1][a * 64 : a * 64 + 64] for a in range(3) if 0 <= out + a - 1 < 4]
        sums.append(functools.reduce(jnp.add, terms))
    return sums


def fine_own(vol, w1, acc, wt, high, low):
    zeros = jnp.zeros((64, 256), BF16)
    for lead in range(2):
        for h in range(4):
            high[lead, h * 256 + 192 : h * 256 + 256, :] = zeros
            low[lead, h * 256 + 192 : h * 256 + 256, :] = zeros
    for b in range(3):
        wt[:, b * 256 + 192 : b * 256 + 256] = jnp.zeros((384, 64), BF16)
    for a in range(3):
        for b in range(3):
            x = w1[a * 576 + b * 192 : a * 576 + b * 192 + 192, :]
            x = jnp.concatenate([x, jnp.zeros((64, 64), F32)], axis=0)
            hi, lo = split(x.T)
            wt[a * 64 : a * 64 + 64, b * 256 : b * 256 + 256] = hi
            wt[192 + a * 64 : 192 + a * 64 + 64, b * 256 : b * 256 + 256] = lo
    for d in range(4):
        for h in range(4):
            put_shifted(vol[pl.ds(d * 4 + h, 64, stride=16), :], high, low, d // 2, h * 256, d % 2 * 128)
    for h in range(4):
        first, last = max(h - 1, 0), min(h + 1, 3)
        rows = slice(first * 256, last * 256 + 256)
        lanes = slice((first - h + 1) * 256, (last - h + 2) * 256)
        weights = wt[:, lanes]
        parts = [taps(weights, high[lead, rows, :], low[lead, rows, :]) for lead in range(2)]
        for i, value in enumerate(planes(*parts)):
            acc[i * 256 + h * 64 : i * 256 + h * 64 + 64, :] = value


def fine_rim(acc, wt, near, far, inner, out_near, out_far, high, low):
    zeros = jnp.zeros((64, 256), BF16)
    for side in range(2):
        for lead in range(2):
            high[side * 2 + lead, 192:256, :] = zeros
            low[side * 2 + lead, 192:256, :] = zeros
    for d in range(4):
        below, above = received(near, far, pl.ds(d * 64, 64), "grp")
        put_shifted(below, high, low, d // 2, 0, d % 2 * 128)
        put_shifted(above, high, low, 2 + d // 2, 0, d % 2 * 128)
    for side in range(2):
        h = (0, 3)[side]
        weights = wt[:, side * 512 : side * 512 + 256]
        parts = [taps(weights, high[side * 2 + lead], low[side * 2 + lead]) for lead in range(2)]
        totals = planes(*parts)
        for i, value in enumerate(totals):
            totals[i] = value + acc[i * 256 + h * 64 : i * 256 + h * 64 + 64, :]
            if 0 < i < 5:
                inner[(i - 1) * 128 + side * 64 : (i - 1) * 128 + side * 64 + 64, :] = totals[i]
        send(out_near, out_far, pl.ds(h * 64, 64), totals[5], totals[0], "slab")
    for h in (1, 2):
        at = pl.ds(h * 64, 64)
        send(out_near, out_far, at, acc[5 * 256 + h * 64 : 5 * 256 + h * 64 + 64, :], acc[at, :], "slab")
    out_far[256:, :] = jnp.zeros((8, 128), F32)


def first_down(acc, inner, near, far, w, out_low, out_high, out_near, out_far, cells, whi, wlo):
    for a in range(2):
        for bk in range(4):
            hi, lo = split(w[(a * 4 + bk) * 64 : (a * 4 + bk) * 64 + 64, :])
            whi[(bk * 2 + a) * 64 : (bk * 2 + a) * 64 + 64, :] = hi
            wlo[(bk * 2 + a) * 64 : (bk * 2 + a) * 64 + 64, :] = lo
    for h in range(4):
        before, after = received(near, far, pl.ds(h * 64, 64), "slab")
        level = []
        for d in range(4):
            if h in (0, 3):
                at = d * 128 + (h == 3) * 64
                v = inner[at : at + 64, :]
            else:
                at = (d + 1) * 256 + h * 64
                v = acc[at : at + 64, :]
            if d == 0:
                v = v + before
            if d == 3:
                v = v + after
            level.append(gelu(v))
        for d2 in range(2):
            cells[h * 2 + d2] = jnp.concatenate(level[2 * d2 : 2 * d2 + 2], axis=0).T
    results = []
    for h2 in range(2):
        rows = []
        for d2 in range(2):
            rows.append(jnp.concatenate(
                [cells[(2 * h2 + b) * 2 + d2, pl.ds(k, 64, stride=2), :] for b in range(2) for k in range(2)], axis=1))
        hi, lo = split(jnp.concatenate(rows, axis=0))
        both = mm(jnp.concatenate([hi, lo], axis=0), whi[...])
        results.append(both[:128] + both[128:] + mm(hi, wlo[...]))
    out_low[...], out_high[...] = results
    send(out_near, out_far, pl.ds(0, 128), results[1], results[0], "grp")
    out_near[128:, :] = jnp.zeros((8, 128), F32)


def filters(wm, wc, mid, coarse):
    for a in range(3):
        for i in range(9):
            x = wm[(a * 9 + i) * 128 : (a * 9 + i) * 128 + 128, :]
            hi, lo = split(x)
            mid[i * 128 : i * 128 + 128, a * 128 : a * 128 + 128] = hi
            mid[1152 + i * 128 : 1152 + i * 128 + 128, a * 128 : a * 128 + 128] = lo
            hi, lo = split(wc[(a * 9 + i) * 64 : (a * 9 + i) * 64 + 64, :])
            coarse[a * 64 : a * 64 + 64, i * 256 : i * 256 + 256] = hi
            coarse[192 + a * 64 : 192 + a * 64 + 64, i * 256 : i * 256 + 256] = lo


def gathered_filters(mine, other, whi, wlo):
    grp = lax.axis_index("grp")
    part = lax.rem(lax.axis_index("slab"), 2)
    for ref, half in ((mine, part), (other, 1 - part)):
        for j, mask in enumerate(XORS):
            at = pl.multiple_of((grp ^ mask) * 32, 32)
            for i in range(4):
                hi, lo = split(ref[j * 128 + i * 32 : j * 128 + i * 32 + 32, :])
                whi[half, pl.ds(at, 32), i * 128 : i * 128 + 128] = hi
                wlo[half, pl.ds(at, 32), i * 128 : i * 128 + 128] = lo


def shifted_rows(x, k, width):
    row = lax.rem(lax.broadcasted_iota(jnp.int32, x.shape, 0), width)
    if k == 0:
        return jnp.where(row == 0, 0.0, pltpu.roll(x, 1, 0))
    if k == 2:
        return jnp.where(row == width - 1, 0.0, pltpu.roll(x, x.shape[0] - 1, 0))
    return x


def put_rows(x, high, low, lead, row):
    for k in range(3):
        hi, lo = split(shifted_rows(x, k, 64))
        high[lead, row : row + 64, k * 128 : k * 128 + 128] = hi
        low[lead, row : row + 64, k * 128 : k * 128 + 128] = lo


def middle_taps(high, low, leads, rows, w, b):
    hi = [high[lead, rows, :] for lead in leads]
    lo = [low[lead, rows, :] for lead in leads]
    n = sum(x.shape[0] for x in hi)
    both = mm(jnp.concatenate(hi + lo, axis=0), w[b * 384 : b * 384 + 384, :])
    return both[:n] + both[n:] + mm(jnp.concatenate(hi, axis=0), w[1152 + b * 384 : 1152 + b * 384 + 384, :])


def middle_own(d_low, d_high, w, total, high, low):
    for i, ref in enumerate((d_low, d_high)):
        for d in range(2):
            put_rows(ref[d * 64 : d * 64 + 64, :], high, low, i, d * 64)
    every = slice(0, 128)
    center = middle_taps(high, low, (0, 1), every, w, 1)
    total[:128, :] = center[:128] + middle_taps(high, low, (1,), every, w, 2)
    total[128:, :] = center[128:] + middle_taps(high, low, (0,), every, w, 0)


def middle_rim(own, near, far, w, inner, out_near, out_far, high, low):
    for d in range(2):
        below, above = received(near, far, pl.ds(d * 64, 64), "grp")
        put_rows(below, high, low, 0, d * 64)
        put_rows(above, high, low, 1, d * 64)
    every = slice(0, 128)
    for h in range(2):
        total = own[h * 128 : h * 128 + 128, :] + middle_taps(high, low, (h,), every, w, 2 * h)
        inner[h * 64 : h * 64 + 64, :] = total[:64, 128:256] + total[64:, 256:]
        inner[128 + h * 64 : 128 + h * 64 + 64, :] = total[:64, :128] + total[64:, 128:256]
        send(out_near, out_far, pl.ds(h * 64, 64), total[64:, :128], total[:64, 256:], "slab")


def level_two(inner, near, far, cells):
    before, after = received(near, far, slice(None), "slab")
    cells[:128, :] = gelu(inner[:128, :] + before)
    cells[128:, :] = gelu(inner[128:, :] + after)


def second_down(cells, whi, wlo, out):
    total = jnp.zeros((32, 256), F32)
    for a in range(2):
        x = jnp.concatenate(
            [cells[pl.ds(a * 128 + b * 64 + k, 32, stride=2), :] for b in range(2) for k in range(2)], axis=1)
        hi, lo = split(x)
        both = mm_t(jnp.concatenate([hi, lo], axis=0), whi[a])
        total = total + (both[:32] + both[32:] + mm_t(hi, wlo[a]))
    out[...] = total


def coarse_conv(own, three, two, one, w, mid, out_near, out_far, grid, high, low):
    grp = lax.axis_index("grp")
    for mask, ref in enumerate((own, one, two, three)):
        for j in range(2):
            at = pl.multiple_of((grp ^ (mask + 4 * j)) * 32, 32)
            grid[pl.ds(at, 32), :] = ref[j * 32 : j * 32 + 32, :]
    zeros = jnp.zeros((32, 768), BF16)
    for ref in (high, low):
        ref[:32, :] = zeros
        ref[288:, :] = zeros
    for k in range(3):
        hi, lo = split(shifted_rows(grid[...], k, 32))
        high[32:288, k * 256 : k * 256 + 256] = hi
        low[32:288, k * 256 : k * 256 + 256] = lo
    total = jnp.zeros((192, 256), F32)
    for b in range(3):
        rows, lanes = slice(b * 32, b * 32 + 256), slice(b * 768, b * 768 + 768)
        both = mm_t(w[:, lanes], high[rows, :])
        total = total + (both[:192] + both[192:] + mm_t(w[:192, lanes], low[rows, :]))
    mid[...] = total[64:128]
    send(out_near, out_far, slice(None), total[:64], total[128:], "slab")


def finish(mid, near, far, out):
    before, after = received(near, far, slice(None), "slab")
    v = gelu(mid[...] + before + after)
    for j in range(2):
        out[pl.ds(j, 64, stride=2), :] = v[:, j * 128 : j * 128 + 128]


def per_device(volume, conv_fine, down_first, conv_middle, down_second, conv_coarse):
    slabs, grps = lax.axis_size("slab"), lax.axis_size("grp")

    def permute(x, target):
        pairs = []
        for s in range(slabs):
            for g in range(grps):
                t, u = target(s, g)
                pairs.append((s * grps + g, t * grps + u))
        return lax.ppermute(x, ("slab", "grp"), pairs)

    def far_slab(s, g):
        if s in (0, slabs - 1):
            return s, g ^ 1
        return (s + 1 if s % 2 else s - 1), g

    def far_grp(s, g):
        if g in (0, grps - 1):
            return s ^ 1, g
        return s, (g + 1 if g % 2 else g - 1)

    def over_grp(near, far):
        far = permute(far, far_grp)
        return swap(near, "grp", 1), far

    def over_slab(near, far):
        far = permute(far, far_slab)
        return swap(near, "slab", 1), far

    def swap(x, axis, mask):
        if axis == "slab":
            return permute(x, lambda s, g: (s ^ mask, g))
        return permute(x, lambda s, g: (s, g ^ mask))

    def join(n, first, second, *after, flops=0, more=0):
        outs = [((2 * n + more, first.shape[1]), F32)]
        kernel = functools.partial(joined, n=n)
        return call(kernel, outs, (first, second), after=after, flops=flops)[0]

    vol = volume.reshape(1024, 128)
    w1 = conv_fine.reshape(1728, 64)
    wd1 = down_first.reshape(512, 128)
    wm = conv_middle.reshape(3456, 128)
    w2 = jnp.swapaxes(down_second, 3, 4).reshape(256, 128)
    wc = jnp.swapaxes(conv_coarse, 3, 4).reshape(1728, 256)

    out = call(edges, [((256, 128), F32), ((264, 128), F32)], (vol,))
    (half,) = call(own_half, [((128, 128), F32)], (w2,), after=(out[0],))
    rim = over_grp(*out)
    second = swap(half, "grp", 4)
    taken = [pltpu.VMEM((2, 1024, 256), BF16)] * 2
    acc, wt = call(
        fine_own, [((1536, 128), F32), ((384, 768), BF16)], (vol, w1), taken, flops=10**9, after=(half,))
    mid_w, coarse_w = call(filters, [((2304, 384), BF16), ((384, 2304), BF16)], (wm, wc), flops=10**8, after=(acc,))
    taken = [pltpu.VMEM((4, 256, 256), BF16)] * 2
    inner, *out = call(
        fine_rim, [((512, 128), F32), ((256, 128), F32), ((264, 128), F32)], (acc, wt, *rim), taken, flops=10**8)
    rim = over_slab(*out)
    two = join(128, half, second, inner, flops=10**10, more=32)
    second = swap(two, "grp", 1)

    four = join(256, two, second, *rim)
    second = swap(four, "grp", 3)
    taken = [pltpu.VMEM((8, 128, 128), F32), pltpu.VMEM((512, 128), BF16), pltpu.VMEM((512, 128), BF16)]
    d_low, d_high, *out = call(
        first_down, [((128, 128), F32)] * 2 + [((136, 128), F32), ((128, 128), F32)], (acc, inner, *rim, wd1), taken, flops=10**8, after=(mid_w,))
    rim = over_grp(*out)
    taken = [pltpu.VMEM((2, 128, 384), BF16)] * 2
    (own,) = call(middle_own, [((256, 384), F32)], (d_low, d_high, mid_w), taken, flops=10**8)
    inner, *out = call(
        middle_rim, [((256, 128), F32)] + [((128, 128), F32)] * 2, (own, *rim, mid_w), taken, flops=10000000000)
    rim = over_slab(*out)
    mine = join(512, four, second, inner)
    other = swap(mine, "slab", 1)
    whi, wlo = call(gathered_filters, [((2, 256, 512), BF16)] * 2, (mine, other))
    (cells,) = call(level_two, [((256, 128), F32)], (inner, *rim), flops=10**10)
    (row,) = call(second_down, [((32, 256), F32)], (cells, whi, wlo), flops=10**8)

    pair = join(32, row, swap(row, "grp", 4))
    others = [swap(pair, "grp", mask) for mask in (3, 2, 1)]
    taken = [pltpu.VMEM((256, 256), F32), pltpu.VMEM((320, 768), BF16), pltpu.VMEM((320, 768), BF16)]
    mid, *out = call(coarse_conv, [((64, 256), F32)] * 3, (pair, *others, coarse_w), taken, flops=10**8)
    rim = over_slab(*out)
    return call(finish, [((128, 128), F32)], (mid, *rim))[0].reshape(64, 1, 256)


def solution(mesh):
    placed = (
        P(None, "slab", "grp", None),
        P(),
        P(),
        P(),
        P(None, None, None, None, "grp"),
        P(None, None, None, None, "grp"),
    )
    return jax.shard_map(
        per_device, mesh=mesh, in_specs=placed, out_specs=P("grp", "slab", None), check_vma=False
    )
```
